256 devices in a mesh: grp: 2 (over y_hi), dp: 16 (over y_lo, z), tp: 8 (over x, core).
Axes of the slice: x: 4, y: 4 (y_hi: 2, y_lo: 2; y = y_hi * 2 + y_lo), z: 8, core: 2. Of those that a mesh axis runs over, the one named last changes fastest.
Arguments:
- tiers: bfloat16 [2048, 24576], P('dp', ('grp', 'tp')), may hold values from -6 to 6
- w_merge: bfloat16 [24576, 8192], P(('grp', 'tp'), 'dp'), may hold values from -0.0390625 to 0.0390625
- norm_gain: float32 [8192], P('dp'), may hold values from 0.4 to 1.6
- w_head: bfloat16 [8192, 32000], P('dp', ('grp', 'tp')), may hold values from -0.1875 to 0.1875
- token_ids: int32 [2048], P('dp'), may hold values from 0 to 31999
- labels: int32 [2048], P('dp'), may hold values from 0 to 7
- quotas: int32 [8], replicated, may hold values from 64 to 191
Outputs:
- normed: bfloat16 [2048, 8192], P(('grp', 'tp'), 'dp')
- row_loss: float32 [2048], P('dp')
The draws below stay inside these ranges and needn't reach their ends.
All inputs are finite; a program needn't handle non-finite values.
Results may differ from the reference program's by a relative error of at most 0.008.
Values may be sent and summed in bfloat16 or wider, within the bound.
A program may use at most 64 MiB of HBM per device.

```python
import math
import jax
import jax.numpy as jnp
import numpy as np
from jax import lax

D = 8192
V = 32000
DOMAINS = 8
TOKENS = 2048


def with_ends(values, stream_key, smallest, largest):
    place = [jax.random.randint(jax.random.fold_in(stream_key, axis), (), 0, length) for axis, length in enumerate(values.shape)]
    longest = values.shape.index(max(values.shape))
    neighbour = place[:longest] + [(place[longest] + 1) % values.shape[longest]] + place[longest + 1:]
    return values.at[tuple(place)].set(smallest).at[tuple(neighbour)].set(largest)


def block_levels(stream_key, extent, pieces, smallest, largest):
    loudness = 1.0
    for dim, shards_of in pieces:
        steps = jax.random.uniform(jax.random.fold_in(jax.random.fold_in(stream_key, 6), dim), (shards_of,), jnp.float32, smallest / len(pieces), largest / len(pieces))
        loudness = loudness * jnp.repeat(jnp.exp(steps), extent[dim] // shards_of).reshape((-1,) + (1,) * (len(extent) - 1 - dim))
    return loudness


def rank_bounds(number_of, skew):
    portions = [(1 << 20) // math.isqrt(standing ** skew) + 1 for standing in range(1, number_of + 1)]
    width = 1 + sum(portions) // (1 << 30)
    return np.cumsum(np.array([max(1, weight // width) for weight in portions]))


def ranked(own_key, shape, count, slope):
    table = rank_bounds(count, slope)
    ticket = jax.random.randint(jax.random.fold_in(own_key, 1), shape, 0, int(table[count - 1]))
    standing = jnp.searchsorted(jnp.asarray(table, jnp.int32), ticket, side="right")
    return jax.random.permutation(jax.random.fold_in(own_key, 2), count)[standing].astype(jnp.int32)


def bell_draw(key, extent, spread, reach, shards=(), kind=jnp.bfloat16):
    values = spread * jax.random.normal(key, extent, jnp.float32)
    if shards:
        values = values * block_levels(key, extent, shards, -0.22, 0.18)
    return jnp.clip(values, -reach, reach).astype(kind)


def setup_inputs(seed: int = 0) -> dict:
    keys = jax.random.split(jax.random.key(seed), 8)
    tiers = bell_draw(keys[0], (TOKENS, 3 * D), 1.0, 6.0, ((0, 16), (1, 16)))
    w_merge = bell_draw(keys[1], (3 * D, D), (3 * D) ** -0.5, 0.0390625, ((0, 16), (1, 16)))
    norm_gain = jnp.clip(1.0 + 0.12 * jax.random.normal(keys[2], (D,), jnp.float32), 0.4, 1.6)
    w_head = bell_draw(keys[3], (D, V), (D // 9) ** -0.5, 0.1875, ((0, 16), (1, 16)))
    token_ids = with_ends(ranked(keys[4], (TOKENS,), V, 2), jax.random.fold_in(keys[4], 3), 0, V - 1).astype(jnp.int32)
    labels = with_ends(jax.random.randint(keys[5], (TOKENS,), 0, DOMAINS), jax.random.fold_in(keys[5], 1), 0, DOMAINS - 1).astype(jnp.int32)
    quotas = with_ends(jax.random.randint(keys[6], (DOMAINS,), TOKENS // (4 * DOMAINS), 3 * TOKENS // (4 * DOMAINS)), jax.random.fold_in(keys[6], 1), TOKENS // (4 * DOMAINS), (3 * TOKENS // (4 * DOMAINS)) - 1).astype(jnp.int32)
    return {"tiers": tiers, "w_merge": w_merge, "norm_gain": norm_gain, "w_head": w_head, "token_ids": token_ids, "labels": labels, "quotas": quotas}


def reference(tiers, w_merge, norm_gain, w_head, token_ids, labels, quotas):
    merged = jnp.dot(tiers, w_merge, preferred_element_type=jnp.float32)
    squares = lax.optimization_barrier(jnp.mean(merged * merged, axis=1))
    normed = (merged * lax.rsqrt(squares + 1e-05)[:, None] * norm_gain[None, :]).astype(jnp.bfloat16)
    logits = jnp.dot(normed, w_head, preferred_element_type=jnp.float32)
    sumexp = lax.optimization_barrier(jnp.sum(jnp.exp(logits), axis=1))
    target = jnp.take_along_axis(logits, token_ids.astype(jnp.int32)[:, None], axis=1)[:, 0]
    loss = jnp.log(sumexp) - target
    onehot = (labels[:, None] == jnp.arange(DOMAINS, dtype=jnp.int32)[None, :]).astype(jnp.int32)
    earlier = jnp.cumsum(onehot, axis=0) - onehot
    rank = lax.optimization_barrier(jnp.sum(earlier * onehot, axis=1))
    allowed = lax.optimization_barrier(jnp.sum(onehot * quotas[None, :], axis=1))
    row_loss = jnp.where(rank < allowed, loss, jnp.float32(0.0))
    return (normed, row_loss)
```

```python
import jax
import jax.numpy as jnp
from jax import lax
from jax.experimental import pallas as pl
from jax.experimental.pallas import tpu as pltpu
from jax.sharding import PartitionSpec as P

D = 8192
Z = 8
ROWS = 128
FEAT = 1536
COLS = 512
VOC = 2000
Q = 256
SPLIT = (0, 1008, VOC)
STEP = (336, 496)
N_SEMS = 140


class Net:
    def __init__(self, send, recv):
        self.send, self.recv, self.n, self.started = send, recv, 0, {}

    def make(self, src, dst, device, i):
        return pltpu.make_async_remote_copy(
            src_ref=src,
            dst_ref=dst,
            send_sem=self.send.at[i],
            recv_sem=self.recv.at[i],
            device_id=device,
            device_id_type=pl.DeviceIdType.MESH,
        )

    def put(self, src, dst, device):
        i = self.n
        self.n += 1
        copy = self.make(src, dst, device, i)
        copy.start()
        self.started[i] = copy
        return i, device

    def got(self, handle, dst):
        i, device = handle
        self.make(dst, dst, device, i).wait_recv()

    def sent(self, handles):
        for i, _ in handles:
            self.started.pop(i).wait_send()

    def drain(self):
        for copy in self.started.values():
            copy.wait_send()


def kernel(
    tiers, w_merge, gain, w_head, token_ids, labels, quotas,
    normed_out, loss_out,
    T, W, G, WH, LA, S1, R1, K, S2, R2, S3, R3, MG, SQ, N, OR, ES, ER, PB, FB, FR,
    send, recv, local, cross,
):
    g, d, t = (lax.axis_index(a) for a in ("grp", "dp", "tp"))
    yl, z = lax.div(d, Z), lax.rem(d, Z)
    x, c = lax.div(t, 2), lax.rem(t, 2)
    net = Net(send, recv)

    def at_z(step):
        return lax.rem(z + step + 2 * Z, Z)

    def slot(b):
        return lax.rem(b, 2), lax.div(b, 2)

    ring = [{"dp": yl * Z + at_z(1)}, {"dp": yl * Z + at_z(-1)}]
    y_peer = {"dp": (1 - yl) * Z + z}
    core_peer = {"tp": 2 * x + 1 - c}
    grp_peer = {"grp": 1 - g}

    def x_to(o):
        return lax.rem(x + o + 4, 4)

    def x_peer(o):
        return {"tp": 2 * x_to(o) + c}

    keep_local = [
        pltpu.make_async_copy(tiers, T.at[slot(z)], local.at[0]),
        pltpu.make_async_copy(w_merge, W.at[yl], local.at[1]),
        pltpu.make_async_copy(w_head, WH.at[yl], local.at[2]),
    ]
    tier_in = {}

    def half(h):
        return pl.ds(64 * h, 64)

    for h in (0, 1):
        for way in (0, 1):
            tier_in[way, 1, h] = net.put(
                tiers.at[half(h)], T.at[(*slot(z), half(h))], ring[way]
            )
    keep_local[0].start()
    keep_local[1].start()
    w_in = []
    for q in (0, 1):
        cols = pl.ds(Q * q, Q)
        w_in.append(net.put(w_merge.at[:, cols], W.at[yl, :, cols], y_peer))
    G[yl] = jnp.broadcast_to(gain[...], (8, COLS))
    gain_in = net.put(G.at[yl], G.at[yl], y_peer)
    LA[d] = jnp.broadcast_to(labels[...], (8, ROWS))
    label_in = []
    for o in range(1, 16):
        label_in.append(net.put(LA.at[d], LA.at[d], {"dp": lax.rem(d + o, 16)}))
    keep_local[2].start()

    for s in (1, 2, 3, 4):
        for h in (0, 1):
            for way in (0, 1):
                if (way, s, h) not in tier_in:
                    continue
                origin = at_z(-s if way == 0 else s)
                piece = T.at[(*slot(origin), half(h))]
                net.got(tier_in[way, s, h], piece)
                if s < 3 or (s == 3 and h == way):
                    tier_in[way, s + 1, h] = net.put(piece, piece, ring[way])
    keep_local[0].wait()
    keep_local[1].wait()

    def w_of(q):
        j = yl if q < 2 else 1 - yl
        return W[j, :, pl.ds(Q * (q % 2), Q)]

    def product(p, q):
        a = T[p].reshape(4 * ROWS, FEAT)
        return jnp.dot(a, w_of(q), preferred_element_type=jnp.float32)

    in1, in2, in3 = {}, {}, {}

    def stage1(q):
        S1[q] = product(1 - c, q).astype(jnp.bfloat16)
        in1[q] = net.put(S1.at[q], R1.at[q], core_peer)
        K[q] = product(c, q)

    def stage2(q):
        net.got(in1[q], R1.at[q])
        total = K[q] + R1[q].astype(jnp.float32)
        K[q] = total
        S2[q] = total.astype(jnp.bfloat16)
        for o in (1, 2, 3):
            rows = pl.ds(pl.multiple_of(x_to(o) * ROWS, ROWS), ROWS)
            in2[q, o] = net.put(S2.at[q, rows], R2.at[q, o - 1], x_peer(o))

    def stage3(q):
        total = K[q, pl.ds(pl.multiple_of(x * ROWS, ROWS), ROWS)]
        for o in (1, 2, 3):
            net.got(in2[q, o], R2.at[q, o - 1])
            total += R2[q, o - 1].astype(jnp.float32)
        K[q, 0:ROWS] = total
        S3[q] = total.astype(jnp.bfloat16)
        other = pl.ds(pl.multiple_of((1 - g) * 64, 64), 64)
        in3[q] = net.put(S3.at[q, other], R3.at[q], grp_peer)

    squares = []

    def stage4(q):
        net.got(in3[q], R3.at[q])
        mine = pl.ds(pl.multiple_of(g * 64, 64), 64)
        m = K[q, mine] + R3[q].astype(jnp.float32)
        MG[yl if q < 2 else 1 - yl, :, pl.ds(Q * (q % 2), Q)] = m
        m = m * m
        squares.append(m[:, :128] + m[:, 128:])

    def other_columns():
        for q in (0, 1):
            net.got(w_in[q], W.at[1 - yl, :, pl.ds(Q * q, Q)])

    stage1(0)
    stage1(1)
    stage2(0)
    other_columns()
    stage1(2)
    stage2(1)
    stage3(0)
    stage1(3)
    net.sent(w_in)
    wh_in = []
    for h in (0, 1):
        rows = pl.ds(SPLIT[h], SPLIT[h + 1] - SPLIT[h])
        wh_in.append(net.put(w_head.at[rows], WH.at[yl, rows], y_peer))
    stage2(2)
    stage3(1)
    stage4(0)
    stage2(3)
    stage3(2)
    stage4(1)
    stage3(3)
    stage4(2)
    stage4(3)

    SQ[z] = (squares[0] + squares[1]) + (squares[2] + squares[3])
    sq_in = [
        net.put(SQ.at[z], SQ.at[z], {"dp": yl * Z + at_z(o)}) for o in range(1, Z)
    ]
    net.got(gain_in, G.at[1 - yl])
    for o in range(1, Z):
        net.got(sq_in[o - 1], SQ.at[at_z(-o)])
    total = SQ[0]
    for i in range(1, Z):
        total += SQ[i]
    r = lax.rsqrt(jnp.sum(total, axis=1, keepdims=True) / D + 1e-05)

    def part(i, mine, p=c):
        row = g if mine else 1 - g
        return N.at[p, i, pl.ds(pl.multiple_of(row * 64, 64), 64)]

    own = pl.ds(pl.multiple_of(g * 64, 64), 64)
    for j in (0, 1):
        N[c, x, own, pl.ds(COLS * j, COLS)] = (MG[j] * r * G[j, 0:1, :]).astype(
            jnp.bfloat16
        )
    grp_in = net.put(part(x, True), part(x, True), grp_peer)
    x_in, core_in = {}, {}
    for o in (1, 2, 3):
        x_in[o, 0] = net.put(part(x, True), part(x, True), x_peer(o))
    core_in[0, 0] = net.put(part(x, True), part(x, True), core_peer)
    net.got(grp_in, part(x, False))
    for o in (1, 2, 3):
        x_in[o, 1] = net.put(part(x, False), part(x, False), x_peer(o))
    core_in[0, 1] = net.put(part(x, False), part(x, False), core_peer)

    columns = pl.ds(pl.multiple_of(g * COLS, COLS), COLS)
    block = N.at[c, x, :, columns]
    to_block = pltpu.make_async_remote_copy(
        src_ref=block,
        dst_ref=OR,
        send_sem=cross.at[0],
        recv_sem=cross.at[1],
        device_id={"grp": yl, "dp": g * Z + z},
        device_id_type=pl.DeviceIdType.MESH,
    )

    @pl.when(g != yl)
    def _():
        to_block.start()

    for mine in (0, 1):
        for o in (1, 2, 3):
            piece = part(x_to(-o), mine == 0)
            net.got(x_in[o, mine], piece)
            core_in[o, mine] = net.put(piece, piece, core_peer)
    for o in (0, 1, 2, 3):
        for mine in (0, 1):
            net.got(core_in[o, mine], part(x_to(-o), mine == 0, 1 - c))

    keep_local[2].wait()

    def logits_part(b, h, out):
        p, i = slot(b)

        def body(k, _):
            rows = pl.ds(pl.multiple_of(SPLIT[h] + k * STEP[h], 16), STEP[h])
            total = jnp.zeros((STEP[h], ROWS), jnp.float32)
            for j in (0, 1):
                total += lax.dot_general(
                    WH[j, rows, :],
                    N[p, i, :, pl.ds(COLS * j, COLS)],
                    (((1,), (1,)), ((), ())),
                    preferred_element_type=jnp.float32,
                )
            out[rows, :] = total
            return 0

        lax.fori_loop(0, (SPLIT[h + 1] - SPLIT[h]) // STEP[h], body, 0)

    got_wh = [False, False]
    logit_in = {}
    for s in (4, 3, 2, 1):
        for h in (0, 1):
            rows = pl.ds(SPLIT[h], SPLIT[h + 1] - SPLIT[h])
            if not got_wh[h]:
                net.got(wh_in[h], WH.at[1 - yl, rows])
                got_wh[h] = True
            for way in (0, 1):
                if s == 4 and h != way:
                    continue
                logits_part(at_z(s if way == 0 else -s), h, PB.at[way])
                total = PB[way, rows, :]
                if (way, s + 1, h) in logit_in:
                    net.got(logit_in[way, s + 1, h], ER.at[way, s, rows])
                    total += ER[way, s, rows, :].astype(jnp.float32)
                ES[way, s - 1, rows, :] = total.astype(jnp.bfloat16)
                logit_in[way, s, h] = net.put(
                    ES.at[way, s - 1, rows], ER.at[way, s - 1, rows], ring[way]
                )

    for o in range(1, 16):
        net.got(label_in[o - 1], LA.at[lax.rem(d - o + 16, 16)])
    domain = lax.broadcasted_iota(jnp.int32, (8, ROWS), 0)
    counts = jnp.zeros((8, ROWS), jnp.float32)
    for i in range(16):
        counts += jnp.where((LA[i] == domain) & (i < d), 1.0, 0.0)
    onehot = jnp.where(labels[...] == domain, 1.0, 0.0)
    earlier = jnp.where(
        lax.broadcasted_iota(jnp.int32, (ROWS, ROWS), 0)
        < lax.broadcasted_iota(jnp.int32, (ROWS, ROWS), 1),
        1.0,
        0.0,
    )
    before = jnp.dot(
        onehot.astype(jnp.bfloat16),
        earlier.astype(jnp.bfloat16),
        preferred_element_type=jnp.float32,
    ) + jnp.sum(counts, axis=1, keepdims=True)
    rank = jnp.sum(onehot * before, axis=0, keepdims=True)
    allowed = jnp.zeros((1, ROWS), jnp.int32)
    for e in range(8):
        allowed = jnp.where(labels[...] == e, quotas[e], allowed)

    for h in (0, 1):
        logits_part(z, h, PB.at[0])
    offset = (g * 8 + t) * VOC
    for h in (0, 1):
        rows = pl.ds(SPLIT[h], SPLIT[h + 1] - SPLIT[h])
        for way in (0, 1):
            net.got(logit_in[way, 1, h], ER.at[way, 0, rows])

    def summed(k, sums):
        rows = pl.ds(pl.multiple_of(k * 80, 16), 80)
        v = PB[0, rows, :] + ER[0, 0, rows, :].astype(jnp.float32)
        v += ER[1, 0, rows, :].astype(jnp.float32)
        index = offset + k * 80 + lax.broadcasted_iota(jnp.int32, (80, ROWS), 0)
        hit = jnp.where(index == token_ids[...], v, 0.0)
        e = jnp.exp(v)
        return (
            sums[0] + jnp.sum(e.reshape(10, 8, ROWS), axis=0),
            sums[1] + jnp.sum(hit.reshape(10, 8, ROWS), axis=0),
        )

    zero = jnp.zeros((8, ROWS), jnp.float32)
    sums = lax.fori_loop(0, VOC // 80, summed, (zero, zero))
    sumexp, target = (jnp.sum(v, axis=0, keepdims=True) for v in sums)
    pair = jnp.where(domain < 4, sumexp, target)

    FB[0] = pair
    i = net.put(FB.at[0], FR.at[0], core_peer)
    net.got(i, FR.at[0])
    pair = pair + FR[0]
    FR[1 + x] = pair
    FB[1] = pair
    pair_in = [net.put(FB.at[1], FR.at[1 + x], x_peer(o)) for o in (1, 2, 3)]
    for o in (1, 2, 3):
        net.got(pair_in[o - 1], FR.at[1 + x_to(-o)])
    pair = (FR[1] + FR[2]) + (FR[3] + FR[4])
    FB[2] = pair
    i = net.put(FB.at[2], FR.at[5], grp_peer)
    net.got(i, FR.at[5])
    pair = pair + FR[5]
    loss = jnp.log(pair[0:1]) - pair[4:5]
    loss_out[...] = jnp.where(rank < allowed.astype(jnp.float32), loss, 0.0)

    @pl.when(g != yl)
    def _():
        to_block.wait_send()
        to_block.wait_recv()
        normed_out[...] = OR[...]

    @pl.when(g == yl)
    def _():
        normed_out[...] = N[c, x, :, columns]

    net.drain()


def on_device(tiers, w_merge, norm_gain, w_head, token_ids, labels, quotas):
    f32, bf16, i32 = jnp.float32, jnp.bfloat16, jnp.int32
    vmem = pl.BlockSpec(memory_space=pltpu.VMEM)
    hbm = pl.BlockSpec(memory_space=pl.ANY)
    normed, loss = pl.pallas_call(
        kernel,
        out_shape=(
            jax.ShapeDtypeStruct((ROWS, COLS), bf16),
            jax.ShapeDtypeStruct((1, ROWS), f32),
        ),
        in_specs=[
            hbm, hbm, vmem, hbm, vmem, vmem, pl.BlockSpec(memory_space=pltpu.SMEM),
        ],
        out_specs=(vmem, vmem),
        scratch_shapes=[
            pltpu.VMEM((2, 4, ROWS, FEAT), bf16),
            pltpu.VMEM((2, FEAT, COLS), bf16),
            pltpu.VMEM((2, 8, COLS), f32),
            pltpu.VMEM((2, VOC, COLS), bf16),
            pltpu.VMEM((16, 8, ROWS), i32),
            pltpu.VMEM((4, 4 * ROWS, Q), bf16),
            pltpu.VMEM((4, 4 * ROWS, Q), bf16),
            pltpu.VMEM((4, 4 * ROWS, Q), f32),
            pltpu.VMEM((4, 4 * ROWS, Q), bf16),
            pltpu.VMEM((4, 3, ROWS, Q), bf16),
            pltpu.VMEM((4, ROWS, Q), bf16),
            pltpu.VMEM((4, 64, Q), bf16),
            pltpu.VMEM((2, 64, COLS), f32),
            pltpu.VMEM((Z, 64, 128), f32),
            pltpu.VMEM((2, 4, ROWS, 2 * COLS), bf16),
            pltpu.VMEM((ROWS, COLS), bf16),
            pltpu.VMEM((2, 4, VOC, ROWS), bf16),
            pltpu.VMEM((2, 4, VOC, ROWS), bf16),
            pltpu.VMEM((2, VOC, ROWS), f32),
            pltpu.VMEM((3, 8, ROWS), f32),
            pltpu.VMEM((6, 8, ROWS), f32),
            pltpu.SemaphoreType.DMA((N_SEMS,)),
            pltpu.SemaphoreType.DMA((N_SEMS,)),
            pltpu.SemaphoreType.DMA((3,)),
            pltpu.SemaphoreType.DMA((2,)),
        ],
        compiler_params=pltpu.CompilerParams(
            has_side_effects=True, vmem_limit_bytes=56 * 2**20
        ),
    )(
        tiers,
        w_merge,
        norm_gain.reshape(1, COLS),
        w_head.T,
        token_ids.reshape(1, ROWS),
        labels.reshape(1, ROWS),
        quotas,
    )
    return normed, loss.reshape(ROWS)


def solution(mesh):
    both = ("grp", "tp")
    in_specs = (
        P("dp", both),
        P(both, "dp"),
        P("dp"),
        P("dp", both),
        P("dp"),
        P("dp"),
        P(),
    )
    out_specs = (P(both, "dp"), P("dp"))
    return jax.shard_map(
        on_device, mesh=mesh, in_specs=in_specs, out_specs=out_specs, check_vma=False
    )
```

```python
import jax
import jax.numpy as jnp
from jax import lax
from jax.experimental import pallas as pl
from jax.experimental.pallas import tpu as pltpu
from jax.sharding import PartitionSpec as P

D = 8192
Z = 8
ROWS = 128
FEAT = 1536
COLS = 512
VOC = 2000
MINE = 1008
SHIFT = VOC - MINE
SPLIT = (0, 528, MINE)
PIECES = (0, 272, 528, 768, MINE)
N_SEMS = 140
DISTANCE = (0, 1, -1, 2, -2, 3, -3, 4)
POS = {s: i for i, s in enumerate(DISTANCE)} | {-4: 7}


class Net:
    def __init__(self, send, recv):
        self.send, self.recv, self.n, self.started = send, recv, 0, {}

    def make(self, src, dst, device, i):
        return pltpu.make_async_remote_copy(
            src_ref=src,
            dst_ref=dst,
            send_sem=self.send.at[i],
            recv_sem=self.recv.at[i],
            device_id=device,
            device_id_type=pl.DeviceIdType.MESH,
        )

    def put(self, src, dst, device):
        i = self.n
        self.n += 1
        copy = self.make(src, dst, device, i)
        copy.start()
        self.started[i] = copy
        return i, device

    def got(self, handle, dst):
        i, device = handle
        self.make(dst, dst, device, i).wait_recv()

    def sent(self, handles):
        for i, _ in handles:
            self.started.pop(i).wait_send()

    def drain(self):
        for copy in self.started.values():
            copy.wait_send()


def kernel(
    tiers, w_merge, gain, w_head, token_ids, labels, quotas,
    normed_out, loss_out,
    T, W, G, TK, WH, LA, S1, R1, PP, S2, R2, S3, R3, SA, SQ, CB, RC, N, ES, ER, PB, FB, FR,
    send, recv, local,
):
    f32, bf16 = jnp.float32, jnp.bfloat16
    g, d, t = (lax.axis_index(a) for a in ("grp", "dp", "tp"))
    yl, z = lax.div(d, Z), lax.rem(d, Z)
    x, c = lax.div(t, 2), lax.rem(t, 2)
    net = Net(send, recv)

    def at_z(step):
        return lax.rem(z + step + 2 * Z, Z)

    ring = [{"dp": yl * Z + at_z(1)}, {"dp": yl * Z + at_z(-1)}]
    y_peer = {"dp": (1 - yl) * Z + z}
    y_other = {"grp": 1 - g, "dp": (1 - yl) * Z + z}
    core_peer = {"tp": 2 * x + 1 - c}
    grp_peer = {"grp": 1 - g}

    def x_to(o):
        return lax.rem(x + o + 4, 4)

    def x_peer(o):
        return {"tp": 2 * x_to(o) + c}

    def dp_peer(o):
        return {"dp": lax.rem(d + o, 16)}

    def lines(start, size):
        return pl.ds(pl.multiple_of(start, 16), size)

    barrier = pltpu.get_barrier_semaphore()
    peers = [core_peer, grp_peer, y_other]
    peers += [x_peer(o) for o in (1, 2, 3)] + [dp_peer(o) for o in range(1, 16)]
    for peer in peers:
        pl.semaphore_signal(
            barrier, inc=1, device_id=peer, device_id_type=pl.DeviceIdType.MESH
        )
    own_head = w_head.at[lines(yl * SHIFT, MINE)]
    keep_local = [
        pltpu.make_async_copy(tiers, T.at[0], local.at[0]),
        pltpu.make_async_copy(w_merge, W.at[0], local.at[1]),
        pltpu.make_async_copy(own_head, WH.at[0], local.at[2]),
    ]
    for copy in keep_local:
        copy.start()
    G[0] = jnp.broadcast_to(gain[...], (8, COLS))
    TK[0] = jnp.broadcast_to(token_ids[...], (8, ROWS))
    LA[d] = jnp.broadcast_to(labels[...], (8, ROWS))
    SA[...] = jnp.zeros_like(SA)
    pl.semaphore_wait(barrier, len(peers))

    def half(h):
        return pl.ds(64 * h, 64)

    def from_way(way, s):
        return POS[-s if way == 0 else s]

    tier_in = {}
    for h in (0, 1):
        for way in (0, 1):
            tier_in[way, 1, h] = net.put(
                tiers.at[half(h)], T.at[from_way(way, 1), half(h)], ring[way]
            )
    w_in = []
    for q in (0, 1):
        cols = pl.ds(256 * q, 256)
        w_in.append(net.put(w_merge.at[:, cols], W.at[1, :, cols], y_peer))
    gain_in = net.put(G.at[0], G.at[1], y_peer)
    token_in = net.put(TK.at[0], TK.at[1], y_peer)
    label_in = [net.put(LA.at[d], LA.at[d], dp_peer(o)) for o in range(1, 16)]

    def ring_step(s, h):
        for way in (0, 1):
            if (way, s, h) in tier_in:
                piece = T.at[from_way(way, s), half(h)]
                net.got(tier_in[way, s, h], piece)
                if s < 3 or (s == 3 and h == way):
                    to = T.at[from_way(way, s + 1), half(h)]
                    tier_in[way, s + 1, h] = net.put(piece, to, ring[way])

    batches = {
        "a": (0, 0, 3, 0, COLS),
        "b": (0, 3, 7, 0, COLS),
        "c": (0, 7, 8, 0, COLS),
        "d": (1, 0, 8, 0, 256),
        "e": (1, 0, 8, 256, COLS),
    }
    in1, in2, in3, inx, inc, iny, inf = {}, {}, {}, {}, {}, {}, {}
    mine, others = lines(c * 64, 64), lines((1 - c) * 64, 64)
    strip = lines(c * 64 + x * 16, 16)

    def stage1(k):
        w, p0, p1, c0, c1 = batches[k]
        n = p1 - p0
        a = T[p0:p1].reshape(n * ROWS, FEAT)
        v = jnp.dot(a, W[w, :, c0:c1], preferred_element_type=f32)
        PP[w, p0:p1, :, c0:c1] = v.reshape(n, ROWS, c1 - c0)
        S1[w, p0:p1, :, c0:c1] = PP[w, p0:p1, others, c0:c1].astype(bf16)
        at = (w, pl.ds(p0, n), slice(None), pl.ds(c0, c1 - c0))
        in1[k] = net.put(S1.at[at], R1.at[at], core_peer)

    def stage2(k):
        w, p0, p1, c0, c1 = batches[k]
        at = (w, pl.ds(p0, p1 - p0), slice(None), pl.ds(c0, c1 - c0))
        net.got(in1[k], R1.at[at])
        PP[w, p0:p1, mine, c0:c1] += R1[w, p0:p1, :, c0:c1].astype(f32)
        for o in (1, 2, 3):
            rows = lines(c * 64 + x_to(o) * 16, 16)
            S2[o - 1, w, p0:p1, :, c0:c1] = PP[w, p0:p1, rows, c0:c1].astype(bf16)
            in2[k, o] = net.put(
                S2.at[(o - 1, *at)], R2.at[(o - 1, *at)], x_peer(o)
            )

    def stage3(k):
        w, p0, p1, c0, c1 = batches[k]
        at = (w, pl.ds(p0, p1 - p0), slice(None), pl.ds(c0, c1 - c0))
        v = PP[w, p0:p1, strip, c0:c1]
        for o in (1, 2, 3):
            net.got(in2[k, o], R2.at[(o - 1, *at)])
            v += R2[o - 1, w, p0:p1, :, c0:c1].astype(f32)
        S3[w, p0:p1, :, c0:c1] = v.astype(bf16)
        in3[k] = net.put(S3.at[at], R3.at[at], grp_peer)

    def stage4(k):
        w, p0, p1, c0, c1 = batches[k]
        at = (w, pl.ds(p0, p1 - p0), slice(None), pl.ds(c0, c1 - c0))
        net.got(in3[k], R3.at[at])
        v = S3[w, p0:p1, :, c0:c1].astype(f32) + R3[w, p0:p1, :, c0:c1].astype(f32)
        N[w, p0:p1, strip, c0:c1] = (v * G[w, 0:1, c0:c1]).astype(bf16)
        v = v * v
        fold = sum(v[:, :, i : i + 128] for i in range(0, c1 - c0, 128))
        for p in range(p0, p1):
            SA[at_z(DISTANCE[p])] += fold[p - p0]
        piece = N.at[w, pl.ds(p0, p1 - p0), strip, pl.ds(c0, c1 - c0)]
        for o in (1, 2, 3):
            inx[k, o] = net.put(piece, piece, x_peer(o))

    def rows_of(k, rows, other_w=False):
        w, p0, p1, c0, c1 = batches[k]
        w = 1 - w if other_w else w
        return N.at[w, pl.ds(p0, p1 - p0), rows, pl.ds(c0, c1 - c0)]

    there, there_others = lines(ROWS + c * 64, 64), lines(ROWS + (1 - c) * 64, 64)

    def spread(k):
        for o in (1, 2, 3):
            net.got(inx[k, o], rows_of(k, lines(c * 64 + x_to(-o) * 16, 16)))
        inc[k] = net.put(rows_of(k, mine), rows_of(k, mine), core_peer)
        iny[k] = net.put(rows_of(k, mine), rows_of(k, there, True), y_other)

    def spread2(k):
        net.got(iny[k], rows_of(k, there, True))
        piece = rows_of(k, there, True)
        inf[k] = net.put(piece, piece, core_peer)

    def spread3(k):
        net.got(inc[k], rows_of(k, others))
        net.got(inf[k], rows_of(k, there_others, True))

    wh_in = []

    def head_piece(i):
        rows = lines((1 - yl) * SHIFT + PIECES[i], PIECES[i + 1] - PIECES[i])
        to = WH.at[1, pl.ds(PIECES[i], PIECES[i + 1] - PIECES[i])]
        wh_in.append(net.put(w_head.at[rows], to, y_peer))

    ring_step(1, 0)
    ring_step(1, 1)
    keep_local[0].wait()
    keep_local[1].wait()
    stage1("a")
    ring_step(2, 0)
    stage2("a")
    ring_step(2, 1)
    stage3("a")
    ring_step(3, 0)
    stage4("a")
    ring_step(3, 1)
    stage1("b")
    spread("a")
    ring_step(4, 0)
    ring_step(4, 1)
    stage1("c")
    stage2("b")
    net.got(w_in[0], W.at[1, :, pl.ds(0, 256)])
    stage1("d")
    stage2("c")
    stage3("b")
    net.got(w_in[1], W.at[1, :, pl.ds(256, 256)])
    stage1("e")
    net.sent(w_in)
    head_piece(0)
    stage2("d")
    stage3("c")
    net.got(gain_in, G.at[1])
    stage4("b")
    stage2("e")
    stage3("d")
    stage4("c")
    head_piece(1)
    spread2("a")
    spread("b")
    stage3("e")
    stage4("d")
    spread("c")
    stage4("e")
    head_piece(2)
    spread2("b")
    spread("d")
    spread2("c")

    by_row = SA[...].reshape(ROWS, 128).T
    SQ[z] = jnp.broadcast_to(jnp.sum(by_row, axis=0, keepdims=True), (8, ROWS))
    sq_in = [
        net.put(SQ.at[z], SQ.at[z], {"dp": yl * Z + at_z(o)}) for o in range(1, Z)
    ]
    spread("e")
    head_piece(3)
    spread2("d")
    spread2("e")
    keep_local[2].wait()
    for k in batches:
        spread3(k)

    def logits_part(p, v, out):
        rows = pl.ds(SPLIT[v], SPLIT[v + 1] - SPLIT[v])
        total = None
        for w in (0, 1):
            part = lax.dot_general(
                WH[w, rows, :],
                N[w, p],
                (((1,), (1,)), ((), ())),
                preferred_element_type=f32,
            )
            total = part if total is None else total + part
        out[rows, :] = total

    logit_in = {}

    def logits_step(s, v):
        rows = pl.ds(SPLIT[v], SPLIT[v + 1] - SPLIT[v])
        for way in (0, 1):
            if s == 4 and v != way:
                continue
            logits_part(POS[s if way == 0 else -s], v, PB.at[way])
        for way in (0, 1):
            if s == 4 and v != way:
                continue
            total = PB[way, rows, :]
            if (way, s + 1, v) in logit_in:
                net.got(logit_in[way, s + 1, v], ER.at[way, s, rows])
                total += ER[way, s, rows, :].astype(f32)
            ES[way, s - 1, rows, :] = total.astype(bf16)
            logit_in[way, s, v] = net.put(
                ES.at[way, s - 1, rows], ER.at[way, s - 1, rows], ring[way]
            )

    def got_head(i):
        net.got(wh_in[i], WH.at[1, pl.ds(PIECES[i], PIECES[i + 1] - PIECES[i])])

    got_head(0)
    got_head(1)
    logits_step(4, 0)
    got_head(2)
    got_head(3)
    logits_step(4, 1)
    logits_step(3, 0)
    logits_step(3, 1)

    for o in range(1, Z):
        net.got(sq_in[o - 1], SQ.at[at_z(-o)])
    total = SQ[0]
    for i in range(1, Z):
        total += SQ[i]
    r = lax.rsqrt(total[0:1] / D + 1e-05)
    CB[...] = jnp.broadcast_to(r, (ROWS, ROWS)).T.reshape(8, 16, ROWS)
    for p in range(8):
        RC[0, p, strip, :] = CB[at_z(DISTANCE[p])]
    rx_in = [
        net.put(RC.at[0, :, strip], RC.at[0, :, strip], x_peer(o)) for o in (1, 2, 3)
    ]
    logits_step(2, 0)
    for o in (1, 2, 3):
        net.got(rx_in[o - 1], RC.at[0, :, lines(c * 64 + x_to(-o) * 16, 16)])
    rc_in = net.put(RC.at[0, :, mine], RC.at[0, :, mine], core_peer)
    ry_in = net.put(RC.at[0, :, mine], RC.at[1, :, mine], y_other)
    logits_step(2, 1)
    net.got(ry_in, RC.at[1, :, mine])
    rf_in = net.put(RC.at[1, :, mine], RC.at[1, :, mine], core_peer)
    logits_step(1, 0)
    net.got(rc_in, RC.at[0, :, others])
    net.got(rf_in, RC.at[1, :, others])
    logits_step(1, 1)

    side = lax.rem(g + yl, 2)
    away = lax.rem(t - z + Z, Z)
    far = lax.div(away, 5)
    p = (1 - far) * (2 * away - 1) + far * (16 - 2 * away) + lax.div(Z - away, Z)
    rows = lines(side * ROWS, ROWS)
    normed_out[...] = (N[0, p, rows, :].astype(f32) * RC[side, p][:, 0:1]).astype(bf16)

    for o in range(1, 16):
        net.got(label_in[o - 1], LA.at[lax.rem(d - o + 16, 16)])
    domain = lax.broadcasted_iota(jnp.int32, (8, ROWS), 0)
    counts = jnp.zeros((8, ROWS), f32)
    for i in range(16):
        counts += jnp.where((LA[i] == domain) & (i < d), 1.0, 0.0)
    onehot = jnp.where(labels[...] == domain, 1.0, 0.0)
    earlier = jnp.where(
        lax.broadcasted_iota(jnp.int32, (ROWS, ROWS), 0)
        < lax.broadcasted_iota(jnp.int32, (ROWS, ROWS), 1),
        1.0,
        0.0,
    )
    before = jnp.dot(
        onehot.astype(bf16), earlier.astype(bf16), preferred_element_type=f32
    ) + jnp.sum(counts, axis=1, keepdims=True)
    rank = jnp.sum(onehot * before, axis=0, keepdims=True)
    allowed = jnp.zeros((1, ROWS), jnp.int32)
    for e in range(8):
        allowed = jnp.where(labels[...] == e, quotas[e], allowed)

    for v in (0, 1):
        logits_part(0, v, PB.at[0])
    net.got(token_in, TK.at[1])
    scale = jnp.concatenate([RC[0, 0].T[0:1], RC[1, 0].T[0:1]], axis=1)
    tokens = jnp.concatenate([TK[0, 0:1], TK[1, 0:1]], axis=1)
    first = (g * 8 + t) * VOC + yl * SHIFT
    for v in (0, 1):
        rows = pl.ds(SPLIT[v], SPLIT[v + 1] - SPLIT[v])
        for way in (0, 1):
            net.got(logit_in[way, 1, v], ER.at[way, 0, rows])

    def summed(k, sums):
        rows = pl.ds(pl.multiple_of(k * 48, 16), 48)
        v = PB[0, rows, :] + ER[0, 0, rows, :].astype(f32)
        v = (v + ER[1, 0, rows, :].astype(f32)) * scale
        row = k * 48 + lax.broadcasted_iota(jnp.int32, (48, 2 * ROWS), 0)
        counted = row >= yl * (2 * MINE - VOC)
        hit = jnp.where(counted & (row + first == tokens), v, 0.0)
        e = jnp.where(counted, jnp.exp(v), 0.0)
        return (
            sums[0] + jnp.sum(e.reshape(6, 8, 2 * ROWS), axis=0),
            sums[1] + jnp.sum(hit.reshape(6, 8, 2 * ROWS), axis=0),
        )

    zero = jnp.zeros((8, 2 * ROWS), f32)
    sums = lax.fori_loop(0, MINE // 48, summed, (zero, zero))
    sumexp, target = (jnp.sum(v, axis=0, keepdims=True) for v in sums)
    wide = lax.broadcasted_iota(jnp.int32, (8, 2 * ROWS), 0)
    pair = jnp.where(wide < 4, sumexp, target)

    FB[0] = pair[:, ROWS:]
    i = net.put(FB.at[0], FR.at[0], y_peer)
    net.got(i, FR.at[0])
    pair = pair[:, :ROWS] + FR[0]
    FB[1] = pair
    i = net.put(FB.at[1], FR.at[1], core_peer)
    net.got(i, FR.at[1])
    pair = pair + FR[1]
    FR[2 + x] = pair
    FB[2] = pair
    pair_in = [net.put(FB.at[2], FR.at[2 + x], x_peer(o)) for o in (1, 2, 3)]
    for o in (1, 2, 3):
        net.got(pair_in[o - 1], FR.at[2 + x_to(-o)])
    pair = (FR[2] + FR[3]) + (FR[4] + FR[5])
    FB[3] = pair
    i = net.put(FB.at[3], FR.at[6], grp_peer)
    net.got(i, FR.at[6])
    pair = pair + FR[6]
    loss = jnp.log(pair[0:1]) - pair[4:5]
    loss_out[...] = jnp.where(rank < allowed.astype(f32), loss, 0.0)
    net.drain()


def on_device(tiers, w_merge, norm_gain, w_head, token_ids, labels, quotas):
    f32, bf16, i32 = jnp.float32, jnp.bfloat16, jnp.int32
    vmem = pl.BlockSpec(memory_space=pltpu.VMEM)
    hbm = pl.BlockSpec(memory_space=pl.ANY)
    normed, loss = pl.pallas_call(
        kernel,
        out_shape=(
            jax.ShapeDtypeStruct((ROWS, COLS), bf16),
            jax.ShapeDtypeStruct((1, ROWS), f32),
        ),
        in_specs=[
            hbm, hbm, vmem, hbm, vmem, vmem, pl.BlockSpec(memory_space=pltpu.SMEM),
        ],
        out_specs=(vmem, vmem),
        scratch_shapes=[
            pltpu.VMEM((8, ROWS, FEAT), bf16),
            pltpu.VMEM((2, FEAT, COLS), bf16),
            pltpu.VMEM((2, 8, COLS), f32),
            pltpu.VMEM((2, 8, ROWS), i32),
            pltpu.VMEM((2, MINE, COLS), bf16),
            pltpu.VMEM((16, 8, ROWS), i32),
            pltpu.VMEM((2, 8, 64, COLS), bf16),
            pltpu.VMEM((2, 8, 64, COLS), bf16),
            pltpu.VMEM((2, 8, ROWS, COLS), f32),
            pltpu.VMEM((3, 2, 8, 16, COLS), bf16),
            pltpu.VMEM((3, 2, 8, 16, COLS), bf16),
            pltpu.VMEM((2, 8, 16, COLS), bf16),
            pltpu.VMEM((2, 8, 16, COLS), bf16),
            pltpu.VMEM((8, 16, 128), f32),
            pltpu.VMEM((Z, 8, ROWS), f32),
            pltpu.VMEM((8, 16, ROWS), f32),
            pltpu.VMEM((2, 8, ROWS, 128), f32),
            pltpu.VMEM((2, 8, 2 * ROWS, COLS), bf16),
            pltpu.VMEM((2, 4, MINE, 2 * ROWS), bf16),
            pltpu.VMEM((2, 4, MINE, 2 * ROWS), bf16),
            pltpu.VMEM((2, MINE, 2 * ROWS), f32),
            pltpu.VMEM((4, 8, ROWS), f32),
            pltpu.VMEM((7, 8, ROWS), f32),
            pltpu.SemaphoreType.DMA((N_SEMS,)),
            pltpu.SemaphoreType.DMA((N_SEMS,)),
            pltpu.SemaphoreType.DMA((3,)),
        ],
        compiler_params=pltpu.CompilerParams(
            collective_id=0, has_side_effects=True, vmem_limit_bytes=56 * 2**20
        ),
    )(
        tiers,
        w_merge,
        norm_gain.reshape(1, COLS),
        w_head.T,
        token_ids.reshape(1, ROWS),
        labels.reshape(1, ROWS),
        quotas,
    )
    return normed, loss.reshape(ROWS)


def solution(mesh):
    both = ("grp", "tp")
    in_specs = (
        P("dp", both),
        P(both, "dp"),
        P("dp"),
        P("dp", both),
        P("dp"),
        P("dp"),
        P(),
    )
    out_specs = (P(both, "dp"), P("dp"))
    return jax.shard_map(
        on_device, mesh=mesh, in_specs=in_specs, out_specs=out_specs, check_vma=False
    )
```

```python
import jax
import jax.numpy as jnp
from jax import lax
from jax.experimental import pallas as pl
from jax.experimental.pallas import tpu as pltpu
from jax.sharding import PartitionSpec as P

D = 8192
Z = 8
ROWS = 128
FEAT = 1536
COLS = 512
VOC = 2000
MINE = 1008
SHIFT = VOC - MINE
SPLIT = (0, 528, MINE)
PIECES = (0, 272, 528, 768, MINE)
N_SEMS = 180
DISTANCE = (0, 1, -1, 2, -2, 3, -3, 4)
POS = {s: i for i, s in enumerate(DISTANCE)} | {-4: 7}


class Net:
    def __init__(self, send, recv):
        self.send, self.recv, self.n, self.started = send, recv, 0, {}

    def make(self, src, dst, device, i):
        return pltpu.make_async_remote_copy(
            src_ref=src,
            dst_ref=dst,
            send_sem=self.send.at[i],
            recv_sem=self.recv.at[i],
            device_id=device,
            device_id_type=pl.DeviceIdType.MESH,
        )

    def put(self, src, dst, device):
        i = self.n
        self.n += 1
        copy = self.make(src, dst, device, i)
        copy.start()
        self.started[i] = copy
        return i, device

    def got(self, handle, dst):
        i, device = handle
        self.make(dst, dst, device, i).wait_recv()

    def sent(self, handles):
        for i, _ in handles:
            self.started.pop(i).wait_send()

    def drain(self):
        for copy in self.started.values():
            copy.wait_send()


def kernel(
    tiers, w_merge, gain, w_head, token_ids, labels, quotas,
    normed_out, loss_out,
    T, W, G, TK, WH, LA, S1, R1, PP, S2, R2, S3, R3, SA, SQ, CB, RC, N, ES, ER, PB, FB, FR,
    send, recv, local,
):
    f32, bf16 = jnp.float32, jnp.bfloat16
    g, d, t = (lax.axis_index(a) for a in ("grp", "dp", "tp"))
    yl, z = lax.div(d, Z), lax.rem(d, Z)
    x, c = lax.div(t, 2), lax.rem(t, 2)
    net = Net(send, recv)

    def at_z(step):
        return lax.rem(z + step + 2 * Z, Z)

    ring = [{"dp": yl * Z + at_z(1)}, {"dp": yl * Z + at_z(-1)}]
    y_peer = {"dp": (1 - yl) * Z + z}
    y_other = {"grp": 1 - g, "dp": (1 - yl) * Z + z}
    core_peer = {"tp": 2 * x + 1 - c}
    grp_peer = {"grp": 1 - g}

    def x_to(o):
        return lax.rem(x + o + 4, 4)

    def x_peer(o):
        return {"tp": 2 * x_to(o) + c}

    def dp_peer(o):
        return {"dp": lax.rem(d + o, 16)}

    def lines(start, size):
        return pl.ds(pl.multiple_of(start, 16), size)

    barrier = pltpu.get_barrier_semaphore()
    y_core = {"dp": (1 - yl) * Z + z, "tp": 2 * x + 1 - c}
    peers = [core_peer, grp_peer, y_other, y_core]
    peers += [{"grp": 1 - g, **x_peer(o)} for o in (1, 2, 3)]
    peers += [x_peer(o) for o in (1, 2, 3)] + [dp_peer(o) for o in range(1, 16)]
    for peer in peers:
        pl.semaphore_signal(
            barrier, inc=1, device_id=peer, device_id_type=pl.DeviceIdType.MESH
        )
    own_head = w_head.at[lines(yl * SHIFT, MINE)]
    keep_local = [
        pltpu.make_async_copy(tiers, T.at[0], local.at[0]),
        pltpu.make_async_copy(w_merge, W.at[0], local.at[1]),
        pltpu.make_async_copy(own_head, WH.at[0], local.at[2]),
    ]
    for copy in keep_local:
        copy.start()
    G[0] = jnp.broadcast_to(gain[...], (8, COLS))
    TK[0] = jnp.broadcast_to(token_ids[...], (8, ROWS))
    LA[d] = jnp.broadcast_to(labels[...], (8, ROWS))
    SA[...] = jnp.zeros_like(SA)
    pl.semaphore_wait(barrier, len(peers))

    def half(h):
        return pl.ds(64 * h, 64)

    def from_way(way, s):
        return POS[-s if way == 0 else s]

    tier_in = {}
    for h in (0, 1):
        for way in (0, 1):
            tier_in[way, 1, h] = net.put(
                tiers.at[half(h)], T.at[from_way(way, 1), half(h)], ring[way]
            )
    w_in = []

    def merge_part(i):
        return pl.ds(768 * (i % 2), 768), pl.ds(128 * (i // 2), 128)

    def merge_piece(i):
        rows, cols = merge_part(i)
        w_in.append(net.put(w_merge.at[rows, cols], W.at[1, rows, cols], y_peer))

    def got_merge(i):
        net.got(w_in[i], W.at[(1, *merge_part(i))])

    merge_piece(0)
    merge_piece(1)
    gain_in = net.put(G.at[0], G.at[1], y_peer)
    token_in = net.put(TK.at[0], TK.at[1], y_peer)
    label_in = [net.put(LA.at[d], LA.at[d], dp_peer(o)) for o in range(1, 16)]

    def ring_step(s, h):
        for way in (0, 1):
            if (way, s, h) in tier_in:
                piece = T.at[from_way(way, s), half(h)]
                net.got(tier_in[way, s, h], piece)
                if s < 3 or (s == 3 and h == way):
                    to = T.at[from_way(way, s + 1), half(h)]
                    tier_in[way, s + 1, h] = net.put(piece, to, ring[way])

    batches = {
        "a": (0, 0, 3, 0, COLS),
        "b": (0, 3, 5, 0, COLS),
        "c": (1, 0, 5, 0, 256),
        "d": (0, 5, 7, 0, COLS),
        "e": (0, 7, 8, 0, COLS),
        "f": (1, 5, 8, 0, 256),
        "g": (1, 0, 8, 256, COLS),
    }
    in1, in2, in3, inx, inc, iny, inf = {}, {}, {}, {}, {}, {}, {}
    mine, others = lines(c * 64, 64), lines((1 - c) * 64, 64)
    strip = lines(c * 64 + x * 16, 16)

    def stage1(k):
        w, p0, p1, c0, c1 = batches[k]
        n = p1 - p0
        a = T[p0:p1].reshape(n * ROWS, FEAT)
        v = jnp.dot(a, W[w, :, c0:c1], preferred_element_type=f32)
        PP[w, p0:p1, :, c0:c1] = v.reshape(n, ROWS, c1 - c0)
        S1[w, p0:p1, :, c0:c1] = PP[w, p0:p1, others, c0:c1].astype(bf16)
        at = (w, pl.ds(p0, n), slice(None), pl.ds(c0, c1 - c0))
        in1[k] = net.put(S1.at[at], R1.at[at], core_peer)

    def stage2(k):
        w, p0, p1, c0, c1 = batches[k]
        at = (w, pl.ds(p0, p1 - p0), slice(None), pl.ds(c0, c1 - c0))
        net.got(in1[k], R1.at[at])
        PP[w, p0:p1, mine, c0:c1] += R1[w, p0:p1, :, c0:c1].astype(f32)
        for o in (1, 2, 3):
            rows = lines(c * 64 + x_to(o) * 16, 16)
            S2[o - 1, w, p0:p1, :, c0:c1] = PP[w, p0:p1, rows, c0:c1].astype(bf16)
            in2[k, o] = net.put(
                S2.at[(o - 1, *at)], R2.at[(o - 1, *at)], x_peer(o)
            )

    def stage3(k):
        w, p0, p1, c0, c1 = batches[k]
        at = (w, pl.ds(p0, p1 - p0), slice(None), pl.ds(c0, c1 - c0))
        v = PP[w, p0:p1, strip, c0:c1]
        for o in (1, 2, 3):
            net.got(in2[k, o], R2.at[(o - 1, *at)])
            v += R2[o - 1, w, p0:p1, :, c0:c1].astype(f32)
        S3[w, p0:p1, :, c0:c1] = v.astype(bf16)
        in3[k] = net.put(S3.at[at], R3.at[at], grp_peer)

    def stage4(k):
        w, p0, p1, c0, c1 = batches[k]
        at = (w, pl.ds(p0, p1 - p0), slice(None), pl.ds(c0, c1 - c0))
        net.got(in3[k], R3.at[at])
        v = S3[w, p0:p1, :, c0:c1].astype(f32) + R3[w, p0:p1, :, c0:c1].astype(f32)
        N[w, p0:p1, strip, c0:c1] = (v * G[w, 0:1, c0:c1]).astype(bf16)
        v = v * v
        fold = sum(v[:, :, i : i + 128] for i in range(0, c1 - c0, 128))
        for p in range(p0, p1):
            SA[at_z(DISTANCE[p])] += fold[p - p0]
        piece = N.at[w, pl.ds(p0, p1 - p0), strip, pl.ds(c0, c1 - c0)]
        for o in (1, 2, 3):
            inx[k, o] = net.put(piece, piece, x_peer(o))

    def rows_of(k, rows, other_w=False):
        w, p0, p1, c0, c1 = batches[k]
        w = 1 - w if other_w else w
        return N.at[w, pl.ds(p0, p1 - p0), rows, pl.ds(c0, c1 - c0)]

    there, there_others = lines(ROWS + c * 64, 64), lines(ROWS + (1 - c) * 64, 64)

    def spread(k):
        for o in (1, 2, 3):
            net.got(inx[k, o], rows_of(k, lines(c * 64 + x_to(-o) * 16, 16)))
        inc[k] = net.put(rows_of(k, mine), rows_of(k, mine), core_peer)
        iny[k] = net.put(rows_of(k, mine), rows_of(k, there, True), y_other)

    def spread2(k):
        net.got(iny[k], rows_of(k, there, True))
        piece = rows_of(k, there, True)
        inf[k] = net.put(piece, piece, core_peer)

    def spread3(k):
        net.got(inc[k], rows_of(k, others))
        net.got(inf[k], rows_of(k, there_others, True))

    wh_in = []

    def head_piece(i):
        rows = lines((1 - yl) * SHIFT + PIECES[i], PIECES[i + 1] - PIECES[i])
        to = WH.at[1, pl.ds(PIECES[i], PIECES[i + 1] - PIECES[i])]
        wh_in.append(net.put(w_head.at[rows], to, y_peer))

    ring_step(1, 0)
    merge_piece(2)
    ring_step(1, 1)
    merge_piece(3)
    keep_local[0].wait()
    keep_local[1].wait()
    stage1("a")
    ring_step(2, 0)
    merge_piece(4)
    stage2("a")
    ring_step(2, 1)
    merge_piece(5)
    stage1("b")
    stage3("a")
    ring_step(3, 0)
    merge_piece(6)
    net.got(gain_in, G.at[1])
    for i in range(4):
        got_merge(i)
    stage1("c")
    stage2("b")
    ring_step(3, 1)
    merge_piece(7)
    stage1("d")
    stage4("a")
    stage2("c")
    stage3("b")
    ring_step(4, 0)
    ring_step(4, 1)
    stage1("e")
    stage1("f")
    stage2("d")
    stage3("c")
    spread("a")
    for i in range(4, 8):
        got_merge(i)
    stage1("g")
    head_piece(0)
    stage4("b")
    stage2("e")
    stage2("f")
    stage3("d")
    stage4("c")
    stage2("g")
    spread("b")
    stage3("e")
    stage3("f")
    stage4("d")
    head_piece(1)
    spread("c")
    stage3("g")
    spread2("a")
    stage4("e")
    stage4("f")
    spread2("b")
    spread("d")
    stage4("g")
    head_piece(2)
    spread2("c")
    spread("e")
    spread("f")
    spread2("d")

    by_row = SA[...].reshape(ROWS, 128).T
    SQ[z] = jnp.broadcast_to(jnp.sum(by_row, axis=0, keepdims=True), (8, ROWS))
    sq_in = [
        net.put(SQ.at[z], SQ.at[z], {"dp": yl * Z + at_z(o)}) for o in range(1, Z)
    ]
    spread("g")
    head_piece(3)
    for k in ("e", "f", "g"):
        spread2(k)
    keep_local[2].wait()
    for k in batches:
        spread3(k)

    def logits_part(p, v, out):
        rows = pl.ds(SPLIT[v], SPLIT[v + 1] - SPLIT[v])
        total = None
        for w in (0, 1):
            part = lax.dot_general(
                WH[w, rows, :],
                N[w, p],
                (((1,), (1,)), ((), ())),
                preferred_element_type=f32,
            )
            total = part if total is None else total + part
        out[rows, :] = total

    logit_in = {}

    def logits_step(*parts):
        for s, v, way in parts:
            logits_part(POS[s if way == 0 else -s], v, PB.at[way])
        for s, v, way in parts:
            rows = pl.ds(SPLIT[v], SPLIT[v + 1] - SPLIT[v])
            total = PB[way, rows, :]
            if (way, s + 1, v) in logit_in:
                net.got(logit_in[way, s + 1, v], ER.at[way, s, rows])
                total += ER[way, s, rows, :].astype(f32)
            ES[way, s - 1, rows, :] = total.astype(bf16)
            logit_in[way, s, v] = net.put(
                ES.at[way, s - 1, rows], ER.at[way, s - 1, rows], ring[way]
            )

    def got_head(i):
        net.got(wh_in[i], WH.at[1, pl.ds(PIECES[i], PIECES[i + 1] - PIECES[i])])

    got_head(0)
    got_head(1)
    logits_step((4, 0, 0), (3, 0, 1))
    got_head(2)
    got_head(3)
    logits_step((3, 1, 0), (4, 1, 1))
    logits_step((3, 0, 0), (2, 0, 1))
    logits_step((2, 1, 0), (3, 1, 1))

    for o in range(1, Z):
        net.got(sq_in[o - 1], SQ.at[at_z(-o)])
    total = SQ[0]
    for i in range(1, Z):
        total += SQ[i]
    r = lax.rsqrt(total[0:1] / D + 1e-05)
    CB[...] = jnp.broadcast_to(r, (ROWS, ROWS)).T.reshape(8, 16, ROWS)
    for p in range(8):
        RC[0, p, strip, :] = CB[at_z(DISTANCE[p])]
    rx_in = [
        net.put(RC.at[0, :, strip], RC.at[0, :, strip], x_peer(o)) for o in (1, 2, 3)
    ]
    logits_step((2, 0, 0), (1, 0, 1))
    for o in (1, 2, 3):
        net.got(rx_in[o - 1], RC.at[0, :, lines(c * 64 + x_to(-o) * 16, 16)])
    rc_in = net.put(RC.at[0, :, mine], RC.at[0, :, mine], core_peer)
    ry_in = net.put(RC.at[0, :, mine], RC.at[1, :, mine], y_other)
    logits_step((1, 1, 0), (2, 1, 1))
    net.got(ry_in, RC.at[1, :, mine])
    rf_in = net.put(RC.at[1, :, mine], RC.at[1, :, mine], core_peer)
    logits_step((1, 0, 0))
    net.got(rc_in, RC.at[0, :, others])
    net.got(rf_in, RC.at[1, :, others])
    logits_step((1, 1, 1))

    side = lax.rem(g + yl, 2)
    away = lax.rem(t - z + Z, Z)
    far = lax.div(away, 5)
    p = (1 - far) * (2 * away - 1) + far * (16 - 2 * away) + lax.div(Z - away, Z)
    rows = lines(side * ROWS, ROWS)
    normed_out[...] = (N[0, p, rows, :].astype(f32) * RC[side, p][:, 0:1]).astype(bf16)

    for o in range(1, 16):
        net.got(label_in[o - 1], LA.at[lax.rem(d - o + 16, 16)])
    domain = lax.broadcasted_iota(jnp.int32, (8, ROWS), 0)
    counts = jnp.zeros((8, ROWS), f32)
    for i in range(16):
        counts += jnp.where((LA[i] == domain) & (i < d), 1.0, 0.0)
    onehot = jnp.where(labels[...] == domain, 1.0, 0.0)
    earlier = jnp.where(
        lax.broadcasted_iota(jnp.int32, (ROWS, ROWS), 0)
        < lax.broadcasted_iota(jnp.int32, (ROWS, ROWS), 1),
        1.0,
        0.0,
    )
    before = jnp.dot(
        onehot.astype(bf16), earlier.astype(bf16), preferred_element_type=f32
    ) + jnp.sum(counts, axis=1, keepdims=True)
    rank = jnp.sum(onehot * before, axis=0, keepdims=True)
    allowed = jnp.zeros((1, ROWS), jnp.int32)
    for e in range(8):
        allowed = jnp.where(labels[...] == e, quotas[e], allowed)

    for v in (0, 1):
        logits_part(0, v, PB.at[0])
    net.got(token_in, TK.at[1])
    scale = jnp.concatenate([RC[0, 0].T[0:1], RC[1, 0].T[0:1]], axis=1)
    tokens = jnp.concatenate([TK[0, 0:1], TK[1, 0:1]], axis=1)
    first = (g * 8 + t) * VOC + yl * SHIFT
    for v in (0, 1):
        rows = pl.ds(SPLIT[v], SPLIT[v + 1] - SPLIT[v])
        for way in (0, 1):
            net.got(logit_in[way, 1, v], ER.at[way, 0, rows])

    def summed(k, sums):
        rows = pl.ds(pl.multiple_of(k * 48, 16), 48)
        v = PB[0, rows, :] + ER[0, 0, rows, :].astype(f32)
        v = (v + ER[1, 0, rows, :].astype(f32)) * scale
        row = k * 48 + lax.broadcasted_iota(jnp.int32, (48, 2 * ROWS), 0)
        counted = row >= yl * (2 * MINE - VOC)
        hit = jnp.where(counted & (row + first == tokens), v, 0.0)
        e = jnp.where(counted, jnp.exp(v), 0.0)
        return (
            sums[0] + jnp.sum(e.reshape(6, 8, 2 * ROWS), axis=0),
            sums[1] + jnp.sum(hit.reshape(6, 8, 2 * ROWS), axis=0),
        )

    zero = jnp.zeros((8, 2 * ROWS), f32)
    sums = lax.fori_loop(0, MINE // 48, summed, (zero, zero))
    sumexp, target = (jnp.sum(v, axis=0, keepdims=True) for v in sums)
    wide = lax.broadcasted_iota(jnp.int32, (8, 2 * ROWS), 0)
    pair = jnp.where(wide < 4, sumexp, target)

    FR[c] = pair[:, :ROWS]
    FB[0] = pair[:, :ROWS]
    FB[1] = pair[:, ROWS:]
    near = [
        net.put(FB.at[0], FR.at[c], core_peer),
        net.put(FB.at[1], FR.at[2 + c], y_peer),
        net.put(FB.at[1], FR.at[2 + c], y_core),
    ]
    net.got(near[0], FR.at[1 - c])
    net.got(near[1], FR.at[2 + c])
    net.got(near[2], FR.at[3 - c])
    pair = (FR[0] + FR[1]) + (FR[2] + FR[3])
    at = 4 + 4 * g
    FB[2] = pair
    FR[at + x] = pair
    across = [
        (net.put(FB.at[2], FR.at[at + x], {"grp": g if same else 1 - g, **x_peer(o)}), same, o)
        for same in (True, False)
        for o in range(4)
        if o or not same
    ]
    for handle, same, o in across:
        net.got(handle, FR.at[(at if same else 8 - 4 * g) + x_to(-o)])
    pair = (FR[4] + FR[5]) + (FR[6] + FR[7])
    pair += (FR[8] + FR[9]) + (FR[10] + FR[11])
    loss = jnp.log(pair[0:1]) - pair[4:5]
    loss_out[...] = jnp.where(rank < allowed.astype(f32), loss, 0.0)
    net.drain()


def on_device(tiers, w_merge, norm_gain, w_head, token_ids, labels, quotas):
    f32, bf16, i32 = jnp.float32, jnp.bfloat16, jnp.int32
    vmem = pl.BlockSpec(memory_space=pltpu.VMEM)
    hbm = pl.BlockSpec(memory_space=pl.ANY)
    normed, loss = pl.pallas_call(
        kernel,
        out_shape=(
            jax.ShapeDtypeStruct((ROWS, COLS), bf16),
            jax.ShapeDtypeStruct((1, ROWS), f32),
        ),
        in_specs=[
            hbm, hbm, vmem, hbm, vmem, vmem, pl.BlockSpec(memory_space=pltpu.SMEM),
        ],
        out_specs=(vmem, vmem),
        scratch_shapes=[
            pltpu.VMEM((8, ROWS, FEAT), bf16),
            pltpu.VMEM((2, FEAT, COLS), bf16),
            pltpu.VMEM((2, 8, COLS), f32),
            pltpu.VMEM((2, 8, ROWS), i32),
            pltpu.VMEM((2, MINE, COLS), bf16),
            pltpu.VMEM((16, 8, ROWS), i32),
            pltpu.VMEM((2, 8, 64, COLS), bf16),
            pltpu.VMEM((2, 8, 64, COLS), bf16),
            pltpu.VMEM((2, 8, ROWS, COLS), f32),
            pltpu.VMEM((3, 2, 8, 16, COLS), bf16),
            pltpu.VMEM((3, 2, 8, 16, COLS), bf16),
            pltpu.VMEM((2, 8, 16, COLS), bf16),
            pltpu.VMEM((2, 8, 16, COLS), bf16),
            pltpu.VMEM((8, 16, 128), f32),
            pltpu.VMEM((Z, 8, ROWS), f32),
            pltpu.VMEM((8, 16, ROWS), f32),
            pltpu.VMEM((2, 8, ROWS, 128), f32),
            pltpu.VMEM((2, 8, 2 * ROWS, COLS), bf16),
            pltpu.VMEM((2, 4, MINE, 2 * ROWS), bf16),
            pltpu.VMEM((2, 4, MINE, 2 * ROWS), bf16),
            pltpu.VMEM((2, MINE, 2 * ROWS), f32),
            pltpu.VMEM((3, 8, ROWS), f32),
            pltpu.VMEM((12, 8, ROWS), f32),
            pltpu.SemaphoreType.DMA((N_SEMS,)),
            pltpu.SemaphoreType.DMA((N_SEMS,)),
            pltpu.SemaphoreType.DMA((3,)),
        ],
        compiler_params=pltpu.CompilerParams(
            collective_id=0, has_side_effects=True, vmem_limit_bytes=56 * 2**20
        ),
    )(
        tiers,
        w_merge,
        norm_gain.reshape(1, COLS),
        w_head.T,
        token_ids.reshape(1, ROWS),
        labels.reshape(1, ROWS),
        quotas,
    )
    return normed, loss.reshape(ROWS)


def solution(mesh):
    both = ("grp", "tp")
    in_specs = (
        P("dp", both),
        P(both, "dp"),
        P("dp"),
        P("dp", both),
        P("dp"),
        P("dp"),
        P(),
    )
    out_specs = (P(both, "dp"), P("dp"))
    return jax.shard_map(
        on_device, mesh=mesh, in_specs=in_specs, out_specs=out_specs, check_vma=False
    )
```

```python
import jax
import jax.numpy as jnp
from jax import lax
from jax.experimental import pallas as pl
from jax.experimental.pallas import tpu as pltpu
from jax.sharding import PartitionSpec as P

D = 8192
Z = 8
ROWS = 128
FEAT = 1536
COLS = 512
VOC = 2000
MINE = 1008
SHIFT = VOC - MINE
SPLIT = (0, 528, MINE)
PIECES = (0, 272, 528, 768, MINE)
N_SEMS = 200
DISTANCE = (0, 1, -1, 2, -2, 3, -3, 4)
POS = {s: i for i, s in enumerate(DISTANCE)} | {-4: 7}


class Net:
    def __init__(self, send, recv):
        self.send, self.recv, self.n, self.started = send, recv, 0, {}

    def make(self, src, dst, device, i):
        return pltpu.make_async_remote_copy(
            src_ref=src,
            dst_ref=dst,
            send_sem=self.send.at[i],
            recv_sem=self.recv.at[i],
            device_id=device,
            device_id_type=pl.DeviceIdType.MESH,
        )

    def put(self, src, dst, device):
        i = self.n
        self.n += 1
        assert i < N_SEMS
        copy = self.make(src, dst, device, i)
        copy.start()
        self.started[i] = copy
        return i, device

    def got(self, handle, dst):
        i, device = handle
        self.make(dst, dst, device, i).wait_recv()

    def sent(self, handles):
        for i, _ in handles:
            self.started.pop(i).wait_send()

    def drain(self):
        for copy in self.started.values():
            copy.wait_send()


def kernel(
    tiers, w_merge, gain, w_head, token_ids, labels, quotas,
    normed_out, loss_out,
    T, W, G, TK, WH, LA, S1, R1, PP, S2, R2, S3, R3, SA, SQ, CB, RC, N, ES, ER, PB, FB, FR,
    send, recv, local,
):
    f32, bf16 = jnp.float32, jnp.bfloat16
    g, d, t = (lax.axis_index(a) for a in ("grp", "dp", "tp"))
    yl, z = lax.div(d, Z), lax.rem(d, Z)
    x, c = lax.div(t, 2), lax.rem(t, 2)
    net = Net(send, recv)

    def at_z(step):
        return lax.rem(z + step + 2 * Z, Z)

    ring = [{"dp": yl * Z + at_z(1)}, {"dp": yl * Z + at_z(-1)}]
    y_peer = {"dp": (1 - yl) * Z + z}
    y_other = {"grp": 1 - g, "dp": (1 - yl) * Z + z}
    core_peer = {"tp": 2 * x + 1 - c}
    grp_peer = {"grp": 1 - g}

    def x_to(o):
        return lax.rem(x + o + 4, 4)

    def x_peer(o):
        return {"tp": 2 * x_to(o) + c}

    def lines(start, size):
        return pl.ds(pl.multiple_of(start, 16), size)

    barrier = pltpu.get_barrier_semaphore()
    y_core = {"dp": (1 - yl) * Z + z, "tp": 2 * x + 1 - c}
    peers = [core_peer, grp_peer, y_other, y_core]
    peers += [{"grp": 1 - g, **x_peer(o)} for o in (1, 2, 3)]
    peers += [x_peer(o) for o in (1, 2, 3)] + [*ring, y_peer]
    for peer in peers:
        pl.semaphore_signal(
            barrier, inc=1, device_id=peer, device_id_type=pl.DeviceIdType.MESH
        )
    own_head = w_head.at[lines(yl * SHIFT, MINE)]
    keep_local = [
        pltpu.make_async_copy(tiers, T.at[0], local.at[0]),
        pltpu.make_async_copy(w_merge, W.at[0], local.at[1]),
        pltpu.make_async_copy(own_head, WH.at[0], local.at[2]),
    ]
    for copy in keep_local:
        copy.start()
    G[0] = jnp.broadcast_to(gain[...], (8, COLS))
    TK[0] = jnp.broadcast_to(token_ids[...], (8, ROWS))
    LA[d] = jnp.broadcast_to(labels[...], (8, ROWS))
    SA[...] = jnp.zeros_like(SA)
    pl.semaphore_wait(barrier, len(peers))

    def half(h):
        return pl.ds(64 * h, 64)

    def from_way(way, s):
        return POS[-s if way == 0 else s]

    tier_in = {}
    for h in (0, 1):
        for way in (0, 1):
            tier_in[way, 1, h] = net.put(
                tiers.at[half(h)], T.at[from_way(way, 1), half(h)], ring[way]
            )
    w_in = []

    def merge_part(i):
        return pl.ds(768 * (i % 2), 768), pl.ds(128 * (i // 2), 128)

    def merge_piece(i):
        rows, cols = merge_part(i)
        w_in.append(net.put(w_merge.at[rows, cols], W.at[1, rows, cols], y_peer))

    def got_merge(i):
        net.got(w_in[i], W.at[(1, *merge_part(i))])

    for i in range(3):
        merge_piece(i)
    gain_in = net.put(G.at[0], G.at[1], y_peer)
    token_in = net.put(TK.at[0], TK.at[1], y_peer)
    label_in = {(way, 1): net.put(LA.at[d], LA.at[d], ring[way]) for way in (0, 1)}

    def small_step(buf, first, handles, way, s):
        if (way, s) in handles:
            piece = buf.at[first + at_z(-s if way == 0 else s)]
            net.got(handles[way, s], piece)
            if s < 3 or (s == 3 and way == 0):
                handles[way, s + 1] = net.put(piece, piece, ring[way])

    def ring_step(s, h):
        for way in (0, 1):
            if (way, s, h) in tier_in:
                piece = T.at[from_way(way, s), half(h)]
                net.got(tier_in[way, s, h], piece)
                if s < 3 or (s == 3 and h == way):
                    to = T.at[from_way(way, s + 1), half(h)]
                    tier_in[way, s + 1, h] = net.put(piece, to, ring[way])
        small_step(LA, yl * Z, label_in, h, s)

    batches = {
        "a": (0, 0, 3, 0, COLS),
        "b": (0, 3, 5, 0, COLS),
        "c": (1, 0, 5, 0, 256),
        "d": (0, 5, 7, 0, COLS),
        "e": (0, 7, 8, 0, COLS),
        "f": (1, 5, 7, 0, 256),
        "g": (1, 0, 7, 256, 384),
        "h": (1, 7, 8, 0, 384),
        "i": (1, 0, 8, 384, COLS),
        "ab": (0, 0, 5, 0, COLS),
    }
    in1, in2, in3, inx, inc, iny, inf = {}, {}, {}, {}, {}, {}, {}
    mine, others = lines(c * 64, 64), lines((1 - c) * 64, 64)
    strip = lines(c * 64 + x * 16, 16)

    def stage1(k):
        w, p0, p1, c0, c1 = batches[k]
        n = p1 - p0
        a = T[p0:p1].reshape(n * ROWS, FEAT)
        v = jnp.dot(a, W[w, :, c0:c1], preferred_element_type=f32)
        PP[w, p0:p1, :, c0:c1] = v.reshape(n, ROWS, c1 - c0)
        S1[w, p0:p1, :, c0:c1] = PP[w, p0:p1, others, c0:c1].astype(bf16)
        at = (w, pl.ds(p0, n), slice(None), pl.ds(c0, c1 - c0))
        in1[k] = net.put(S1.at[at], R1.at[at], core_peer)

    def stage2(k):
        w, p0, p1, c0, c1 = batches[k]
        at = (w, pl.ds(p0, p1 - p0), slice(None), pl.ds(c0, c1 - c0))
        net.got(in1[k], R1.at[at])
        PP[w, p0:p1, mine, c0:c1] += R1[w, p0:p1, :, c0:c1].astype(f32)
        for o in (1, 2, 3):
            rows = lines(c * 64 + x_to(o) * 16, 16)
            S2[o - 1, w, p0:p1, :, c0:c1] = PP[w, p0:p1, rows, c0:c1].astype(bf16)
            in2[k, o] = net.put(
                S2.at[(o - 1, *at)], R2.at[(o - 1, *at)], x_peer(o)
            )

    def stage3(k):
        w, p0, p1, c0, c1 = batches[k]
        at = (w, pl.ds(p0, p1 - p0), slice(None), pl.ds(c0, c1 - c0))
        v = PP[w, p0:p1, strip, c0:c1]
        for o in (1, 2, 3):
            net.got(in2[k, o], R2.at[(o - 1, *at)])
            v += R2[o - 1, w, p0:p1, :, c0:c1].astype(f32)
        S3[w, p0:p1, :, c0:c1] = v.astype(bf16)
        in3[k] = net.put(S3.at[at], R3.at[at], grp_peer)

    def stage4(k):
        w, p0, p1, c0, c1 = batches[k]
        at = (w, pl.ds(p0, p1 - p0), slice(None), pl.ds(c0, c1 - c0))
        net.got(in3[k], R3.at[at])
        v = S3[w, p0:p1, :, c0:c1].astype(f32) + R3[w, p0:p1, :, c0:c1].astype(f32)
        N[w, p0:p1, strip, c0:c1] = (v * G[w, 0:1, c0:c1]).astype(bf16)
        v = v * v
        fold = sum(v[:, :, i : i + 128] for i in range(0, c1 - c0, 128))
        for p in range(p0, p1):
            SA[at_z(DISTANCE[p])] += fold[p - p0]
        piece = N.at[w, pl.ds(p0, p1 - p0), strip, pl.ds(c0, c1 - c0)]
        for o in (1, 2, 3):
            inx[k, o] = net.put(piece, piece, x_peer(o))

    there, there_others = lines(ROWS + c * 64, 64), lines(ROWS + (1 - c) * 64, 64)

    def spread(*keys):
        for k in keys:
            w, p0, p1, c0, c1 = batches[k]
            blocks, cols = pl.ds(p0, p1 - p0), pl.ds(c0, c1 - c0)
            for o in (1, 2, 3):
                rows = lines(c * 64 + x_to(-o) * 16, 16)
                net.got(inx[k, o], N.at[w, blocks, rows, cols])
            piece = N.at[w, blocks, mine, cols]
            inc[k] = net.put(piece, piece, core_peer)

    def have_near():
        for k, handle in inc.items():
            w, p0, p1, c0, c1 = batches[k]
            net.got(handle, N.at[w, pl.ds(p0, p1 - p0), others, pl.ds(c0, c1 - c0)])

    def to_far(*keys):
        for k in keys:
            w, p0, p1, c0, c1 = batches[k]
            blocks, cols = pl.ds(p0, p1 - p0), pl.ds(c0, c1 - c0)
            iny[k] = net.put(
                N.at[w, blocks, mine, cols], N.at[1 - w, blocks, there, cols], y_other
            )

    def pass_far(*keys):
        for k in keys:
            w, p0, p1, c0, c1 = batches[k]
            piece = N.at[1 - w, pl.ds(p0, p1 - p0), there, pl.ds(c0, c1 - c0)]
            net.got(iny[k], piece)
            inf[k] = net.put(piece, piece, core_peer)

    def have_far():
        for k, handle in inf.items():
            w, p0, p1, c0, c1 = batches[k]
            blocks, cols = pl.ds(p0, p1 - p0), pl.ds(c0, c1 - c0)
            net.got(handle, N.at[1 - w, blocks, there_others, cols])

    wh_in = []

    def head_piece(i):
        rows = lines((1 - yl) * SHIFT + PIECES[i], PIECES[i + 1] - PIECES[i])
        to = WH.at[1, pl.ds(PIECES[i], PIECES[i + 1] - PIECES[i])]
        wh_in.append(net.put(w_head.at[rows], to, y_peer))

    ring_step(1, 0)
    merge_piece(3)
    ring_step(1, 1)
    merge_piece(4)
    keep_local[0].wait()
    keep_local[1].wait()
    stage1("a")
    stage2("a")
    ring_step(2, 0)
    merge_piece(5)
    stage3("a")
    ring_step(2, 1)
    merge_piece(6)
    stage1("b")
    ring_step(3, 0)
    merge_piece(7)
    stage2("b")
    net.got(gain_in, G.at[1])
    for i in range(4):
        got_merge(i)
    stage1("c")
    ring_step(3, 1)
    stage1("d")
    stage1("f")
    got_merge(4)
    got_merge(5)
    stage1("g")
    stage2("c")
    stage3("b")
    stage4("a")
    for k in ("d", "f", "g"):
        stage2(k)
    ring_step(4, 0)
    ring_step(4, 1)
    stage1("e")
    stage1("h")
    stage3("c")
    got_merge(6)
    got_merge(7)
    stage1("i")
    head_piece(0)
    stage2("e")
    stage2("h")
    for k in ("d", "f", "g"):
        stage3(k)
    stage2("i")
    stage4("b")
    spread("a")
    stage4("c")
    stage3("e")
    stage3("h")
    for k in ("d", "f", "g"):
        stage4(k)
    stage3("i")
    head_piece(1)
    stage4("e")
    stage4("h")
    spread("b")
    spread("c")
    to_far("ab", "c")
    spread("d", "f", "g")
    to_far("d", "f", "g")
    stage4("i")
    head_piece(2)
    head_piece(3)

    by_row = SA[...].reshape(ROWS, 128).T
    SQ[z] = jnp.broadcast_to(jnp.sum(by_row, axis=0, keepdims=True), (8, ROWS))
    square_in = {(way, 1): net.put(SQ.at[z], SQ.at[z], ring[way]) for way in (0, 1)}
    spread("e", "h", "i")
    to_far("e", "h", "i")
    half_labels = LA.at[pl.ds(yl * Z, Z)]
    y_labels = net.put(half_labels, half_labels, y_peer)
    keep_local[2].wait()
    have_near()

    def piece_of(v, far):
        rows = pl.ds(SPLIT[v], SPLIT[v + 1] - SPLIT[v])
        return rows, pl.ds(ROWS * far, ROWS)

    def logits_part(p, v, far, out):
        rows, lanes = piece_of(v, far)
        total = None
        for w in (0, 1):
            part = lax.dot_general(
                WH[w, rows, :],
                N[w, p, lanes, :],
                (((1,), (1,)), ((), ())),
                preferred_element_type=f32,
            )
            total = part if total is None else total + part
        out[rows, lanes] = total

    logit_in = {}

    def logits_step(*parts):
        for way, (s, v, far) in enumerate(parts):
            logits_part(POS[s if way == 0 else -s], v, far, PB.at[way])
        for way, (s, v, far) in enumerate(parts):
            at = piece_of(v, far)
            total = PB[(way, *at)]
            if (way, s + 1, v, far) in logit_in:
                net.got(logit_in[way, s + 1, v, far], ER.at[(way, s, *at)])
                total += ER[(way, s, *at)].astype(f32)
            ES[(way, s - 1, *at)] = total.astype(bf16)
            logit_in[way, s, v, far] = net.put(
                ES.at[(way, s - 1, *at)], ER.at[(way, s - 1, *at)], ring[way]
            )

    def got_head(i):
        net.got(wh_in[i], WH.at[1, pl.ds(PIECES[i], PIECES[i + 1] - PIECES[i])])

    got_head(0)
    got_head(1)
    def squares_step(s):
        for way in (0, 1):
            small_step(SQ, 0, square_in, way, s)

    logits_step((4, 0, 0), (3, 0, 0))
    logits_step((3, 0, 0), (2, 0, 0))
    squares_step(1)
    pass_far("ab", "c")
    got_head(2)
    got_head(3)
    logits_step((3, 1, 0), (4, 1, 0))
    pass_far("d")
    logits_step((2, 0, 0), (1, 0, 0))
    squares_step(2)
    pass_far("f", "g")
    logits_step((2, 1, 0), (3, 1, 0))
    pass_far("e", "h", "i")
    have_far()
    logits_step((4, 0, 1), (4, 1, 1))
    squares_step(3)
    logits_step((1, 0, 0), (2, 1, 0))
    logits_step((1, 1, 0), (3, 0, 1))
    squares_step(4)

    total = SQ[0]
    for i in range(1, Z):
        total += SQ[i]
    r = lax.rsqrt(total[0:1] / D + 1e-05)
    CB[...] = jnp.broadcast_to(r, (ROWS, ROWS)).T.reshape(8, 16, ROWS)
    for p in range(8):
        RC[0, p, strip, :] = CB[at_z(DISTANCE[p])]
    rx_in = [
        net.put(RC.at[0, :, strip], RC.at[0, :, strip], x_peer(o)) for o in (1, 2, 3)
    ]
    logits_step((3, 1, 1), (1, 1, 0))
    logits_step((3, 0, 1), (3, 1, 1))
    for o in (1, 2, 3):
        net.got(rx_in[o - 1], RC.at[0, :, lines(c * 64 + x_to(-o) * 16, 16)])
    rc_in = net.put(RC.at[0, :, mine], RC.at[0, :, mine], core_peer)
    ry_in = net.put(RC.at[0, :, mine], RC.at[1, :, mine], y_other)
    logits_step((2, 1, 1), (2, 0, 1))
    logits_step((2, 0, 1), (2, 1, 1))
    net.got(ry_in, RC.at[1, :, mine])
    rf_in = net.put(RC.at[1, :, mine], RC.at[1, :, mine], core_peer)
    logits_step((1, 1, 1), (1, 0, 1))
    logits_step((1, 0, 1), (1, 1, 1))
    net.got(rc_in, RC.at[0, :, others])
    net.got(rf_in, RC.at[1, :, others])

    side = lax.rem(g + yl, 2)
    away = lax.rem(t - z + Z, Z)
    far = lax.div(away, 5)
    p = (1 - far) * (2 * away - 1) + far * (16 - 2 * away) + lax.div(Z - away, Z)
    rows = lines(side * ROWS, ROWS)
    normed_out[...] = (N[0, p, rows, :].astype(f32) * RC[side, p][:, 0:1]).astype(bf16)

    net.got(y_labels, LA.at[pl.ds((1 - yl) * Z, Z)])
    domain = lax.broadcasted_iota(jnp.int32, (8, ROWS), 0)
    counts = jnp.zeros((8, ROWS), f32)
    for i in range(16):
        counts += jnp.where((LA[i] == domain) & (i < d), 1.0, 0.0)
    onehot = jnp.where(labels[...] == domain, 1.0, 0.0)
    earlier = jnp.where(
        lax.broadcasted_iota(jnp.int32, (ROWS, ROWS), 0)
        < lax.broadcasted_iota(jnp.int32, (ROWS, ROWS), 1),
        1.0,
        0.0,
    )
    before = jnp.dot(
        onehot.astype(bf16), earlier.astype(bf16), preferred_element_type=f32
    ) + jnp.sum(counts, axis=1, keepdims=True)
    rank = jnp.sum(onehot * before, axis=0, keepdims=True)
    allowed = jnp.zeros((1, ROWS), jnp.int32)
    for e in range(8):
        allowed = jnp.where(labels[...] == e, quotas[e], allowed)

    for v in (0, 1):
        for far in (0, 1):
            logits_part(0, v, far, PB.at[0])
    net.got(token_in, TK.at[1])
    scale = [RC[far, 0].T[0:1] for far in (0, 1)]
    first = (g * 8 + t) * VOC + yl * SHIFT
    def sums_of(v, far):
        for way in (0, 1):
            net.got(logit_in[way, 1, v, far], ER.at[(way, 0, *piece_of(v, far))])
        lanes = pl.ds(ROWS * far, ROWS)
        valid = yl * (2 * MINE - VOC)

        def summed(k, sums):
            start = SPLIT[v] + k * 48
            rows = pl.ds(pl.multiple_of(start, 16), 48)
            u = PB[0, rows, lanes] + ER[0, 0, rows, lanes].astype(f32)
            u = (u + ER[1, 0, rows, lanes].astype(f32)) * scale[far]
            row = start + lax.broadcasted_iota(jnp.int32, (48, ROWS), 0)
            counted = row >= valid
            hit = jnp.where(counted & (row + first == TK[far, 0:1]), u, 0.0)
            e = jnp.where(counted, jnp.exp(u), 0.0)
            return (
                sums[0] + jnp.sum(e.reshape(6, 8, ROWS), axis=0),
                sums[1] + jnp.sum(hit.reshape(6, 8, ROWS), axis=0),
            )

        zero = jnp.zeros((8, ROWS), f32)
        return lax.fori_loop(0, (SPLIT[v + 1] - SPLIT[v]) // 48, summed, (zero, zero))

    parts = {at: sums_of(*at) for at in ((1, 0), (0, 0), (0, 1), (1, 1))}
    pairs = []
    for far in (0, 1):
        sumexp, target = (
            jnp.sum(parts[0, far][i] + parts[1, far][i], axis=0, keepdims=True)
            for i in (0, 1)
        )
        pairs.append(jnp.where(domain < 4, sumexp, target))

    FR[c] = pairs[0]
    FB[0] = pairs[0]
    FB[1] = pairs[1]
    near = [
        net.put(FB.at[0], FR.at[c], core_peer),
        net.put(FB.at[1], FR.at[2 + c], y_peer),
        net.put(FB.at[1], FR.at[2 + c], y_core),
    ]
    net.got(near[0], FR.at[1 - c])
    net.got(near[1], FR.at[2 + c])
    net.got(near[2], FR.at[3 - c])
    pair = (FR[0] + FR[1]) + (FR[2] + FR[3])
    at = 4 + 4 * g
    FB[2] = pair
    FR[at + x] = pair
    across = [
        (net.put(FB.at[2], FR.at[at + x], {"grp": g if same else 1 - g, **x_peer(o)}), same, o)
        for same in (True, False)
        for o in range(4)
        if o or not same
    ]
    for handle, same, o in across:
        net.got(handle, FR.at[(at if same else 8 - 4 * g) + x_to(-o)])
    pair = (FR[4] + FR[5]) + (FR[6] + FR[7])
    pair += (FR[8] + FR[9]) + (FR[10] + FR[11])
    loss = jnp.log(pair[0:1]) - pair[4:5]
    loss_out[...] = jnp.where(rank < allowed.astype(f32), loss, 0.0)
    net.drain()


def on_device(tiers, w_merge, norm_gain, w_head, token_ids, labels, quotas):
    f32, bf16, i32 = jnp.float32, jnp.bfloat16, jnp.int32
    vmem = pl.BlockSpec(memory_space=pltpu.VMEM)
    hbm = pl.BlockSpec(memory_space=pl.ANY)
    normed, loss = pl.pallas_call(
        kernel,
        out_shape=(
            jax.ShapeDtypeStruct((ROWS, COLS), bf16),
            jax.ShapeDtypeStruct((1, ROWS), f32),
        ),
        in_specs=[
            hbm, hbm, vmem, hbm, vmem, vmem, pl.BlockSpec(memory_space=pltpu.SMEM),
        ],
        out_specs=(vmem, vmem),
        scratch_shapes=[
            pltpu.VMEM((8, ROWS, FEAT), bf16),
            pltpu.VMEM((2, FEAT, COLS), bf16),
            pltpu.VMEM((2, 8, COLS), f32),
            pltpu.VMEM((2, 8, ROWS), i32),
            pltpu.VMEM((2, MINE, COLS), bf16),
            pltpu.VMEM((16, 8, ROWS), i32),
            pltpu.VMEM((2, 8, 64, COLS), bf16),
            pltpu.VMEM((2, 8, 64, COLS), bf16),
            pltpu.VMEM((2, 8, ROWS, COLS), f32),
            pltpu.VMEM((3, 2, 8, 16, COLS), bf16),
            pltpu.VMEM((3, 2, 8, 16, COLS), bf16),
            pltpu.VMEM((2, 8, 16, COLS), bf16),
            pltpu.VMEM((2, 8, 16, COLS), bf16),
            pltpu.VMEM((8, 16, 128), f32),
            pltpu.VMEM((Z, 8, ROWS), f32),
            pltpu.VMEM((8, 16, ROWS), f32),
            pltpu.VMEM((2, 8, ROWS, 128), f32),
            pltpu.VMEM((2, 8, 2 * ROWS, COLS), bf16),
            pltpu.VMEM((2, 4, MINE, 2 * ROWS), bf16),
            pltpu.VMEM((2, 4, MINE, 2 * ROWS), bf16),
            pltpu.VMEM((2, MINE, 2 * ROWS), f32),
            pltpu.VMEM((3, 8, ROWS), f32),
            pltpu.VMEM((12, 8, ROWS), f32),
            pltpu.SemaphoreType.DMA((N_SEMS,)),
            pltpu.SemaphoreType.DMA((N_SEMS,)),
            pltpu.SemaphoreType.DMA((3,)),
        ],
        compiler_params=pltpu.CompilerParams(
            collective_id=0, has_side_effects=True, vmem_limit_bytes=56 * 2**20
        ),
    )(
        tiers,
        w_merge,
        norm_gain.reshape(1, COLS),
        w_head.T,
        token_ids.reshape(1, ROWS),
        labels.reshape(1, ROWS),
        quotas,
    )
    return normed, loss.reshape(ROWS)


def solution(mesh):
    both = ("grp", "tp")
    in_specs = (
        P("dp", both),
        P(both, "dp"),
        P("dp"),
        P("dp", both),
        P("dp"),
        P("dp"),
        P(),
    )
    out_specs = (P(both, "dp"), P("dp"))
    return jax.shard_map(
        on_device, mesh=mesh, in_specs=in_specs, out_specs=out_specs, check_vma=False
    )
```

```python
import jax
import jax.numpy as jnp
from jax import lax
from jax.experimental import pallas as pl
from jax.experimental.pallas import tpu as pltpu
from jax.sharding import PartitionSpec as P

D = 8192
Z = 8
ROWS = 128
FEAT = 1536
COLS = 512
VOC = 2000
MINE = 1008
SHIFT = VOC - MINE
SPLIT = (0, 528, MINE)
PIECES = (0, 144, 528, 768, MINE)
N_SEMS = 200
DISTANCE = (0, 1, -1, 2, -2, 3, -3, 4)
POS = {s: i for i, s in enumerate(DISTANCE)} | {-4: 7}


class Net:
    def __init__(self, send, recv):
        self.send, self.recv, self.n, self.started = send, recv, 0, {}

    def make(self, src, dst, device, i):
        return pltpu.make_async_remote_copy(
            src_ref=src,
            dst_ref=dst,
            send_sem=self.send.at[i],
            recv_sem=self.recv.at[i],
            device_id=device,
            device_id_type=pl.DeviceIdType.MESH,
        )

    def put(self, src, dst, device):
        i = self.n
        self.n += 1
        assert i < N_SEMS
        copy = self.make(src, dst, device, i)
        copy.start()
        self.started[i] = copy
        return i, device

    def got(self, handle, dst):
        i, device = handle
        self.make(dst, dst, device, i).wait_recv()

    def sent(self, handles):
        for i, _ in handles:
            self.started.pop(i).wait_send()

    def drain(self):
        for copy in self.started.values():
            copy.wait_send()


def kernel(
    tiers, w_merge, gain, w_head, token_ids, labels, quotas,
    normed_out, loss_out,
    T, W, G, TK, WH, LA, S1, R1, PP, S2, R2, S3, R3, SA, SQ, CB, RC, N, ES, ER, PB, FB, FR,
    send, recv, local,
):
    f32, bf16 = jnp.float32, jnp.bfloat16
    g, d, t = (lax.axis_index(a) for a in ("grp", "dp", "tp"))
    yl, z = lax.div(d, Z), lax.rem(d, Z)
    x, c = lax.div(t, 2), lax.rem(t, 2)
    net = Net(send, recv)

    def at_z(step):
        return lax.rem(z + step + 2 * Z, Z)

    ring = [{"dp": yl * Z + at_z(1)}, {"dp": yl * Z + at_z(-1)}]
    y_peer = {"dp": (1 - yl) * Z + z}
    y_other = {"grp": 1 - g, "dp": (1 - yl) * Z + z}
    core_peer = {"tp": 2 * x + 1 - c}
    grp_peer = {"grp": 1 - g}

    def x_to(o):
        return lax.rem(x + o + 4, 4)

    def x_peer(o):
        return {"tp": 2 * x_to(o) + c}

    def lines(start, size):
        return pl.ds(pl.multiple_of(start, 16), size)

    barrier = pltpu.get_barrier_semaphore()
    y_core = {"dp": (1 - yl) * Z + z, "tp": 2 * x + 1 - c}
    peers = [core_peer, grp_peer, y_other, y_core]
    peers += [{"grp": 1 - g, **x_peer(o)} for o in (1, 2, 3)]
    peers += [x_peer(o) for o in (1, 2, 3)] + [*ring, y_peer]
    for peer in peers:
        pl.semaphore_signal(
            barrier, inc=1, device_id=peer, device_id_type=pl.DeviceIdType.MESH
        )
    own_head = w_head.at[lines(yl * SHIFT, MINE)]
    keep_local = [
        pltpu.make_async_copy(tiers, T.at[0], local.at[0]),
        pltpu.make_async_copy(w_merge, W.at[0], local.at[1]),
        pltpu.make_async_copy(own_head, WH.at[0], local.at[2]),
    ]
    for copy in keep_local:
        copy.start()
    G[0] = jnp.broadcast_to(gain[...], (8, COLS))
    TK[0] = jnp.broadcast_to(token_ids[...], (8, ROWS))
    LA[d] = jnp.broadcast_to(labels[...], (8, ROWS))
    SA[...] = jnp.zeros_like(SA)
    pl.semaphore_wait(barrier, len(peers))

    def half(h):
        return pl.ds(64 * h, 64)

    def from_way(way, s):
        return POS[-s if way == 0 else s]

    tier_in = {}
    for h in (0, 1):
        for way in (0, 1):
            tier_in[way, 1, h] = net.put(
                tiers.at[half(h)], T.at[from_way(way, 1), half(h)], ring[way]
            )
    w_in = []

    def merge_part(i):
        return pl.ds(768 * (i % 2), 768), pl.ds(128 * (i // 2), 128)

    def merge_piece(i):
        rows, cols = merge_part(i)
        w_in.append(net.put(w_merge.at[rows, cols], W.at[1, rows, cols], y_peer))

    def got_merge(i):
        net.got(w_in[i], W.at[(1, *merge_part(i))])

    for i in range(3):
        merge_piece(i)
    gain_in = net.put(G.at[0], G.at[1], y_peer)
    token_in = net.put(TK.at[0], TK.at[1], y_peer)
    label_in = {(way, 1): net.put(LA.at[d], LA.at[d], ring[way]) for way in (0, 1)}

    def small_step(buf, first, handles, way, s):
        if (way, s) in handles:
            piece = buf.at[first + at_z(-s if way == 0 else s)]
            net.got(handles[way, s], piece)
            if s < 3 or (s == 3 and way == 0):
                handles[way, s + 1] = net.put(piece, piece, ring[way])

    def ring_step(s, h):
        for way in (0, 1):
            if (way, s, h) in tier_in:
                piece = T.at[from_way(way, s), half(h)]
                net.got(tier_in[way, s, h], piece)
                if s < 3 or (s == 3 and h == way):
                    to = T.at[from_way(way, s + 1), half(h)]
                    tier_in[way, s + 1, h] = net.put(piece, to, ring[way])
        small_step(LA, yl * Z, label_in, h, s)

    batches = {
        "a": (0, 0, 3, 0, COLS),
        "b": (0, 3, 5, 0, COLS),
        "c": (1, 0, 5, 0, 256),
        "d": (0, 5, 7, 0, COLS),
        "e": (0, 7, 8, 0, COLS),
        "f": (1, 5, 7, 0, 256),
        "g": (1, 0, 7, 256, 384),
        "h": (1, 7, 8, 0, 384),
        "i": (1, 0, 8, 384, COLS),
        "ab": (0, 0, 5, 0, COLS),
    }
    in1, in2, in3, inx, inc, iny, inf = {}, {}, {}, {}, {}, {}, {}
    mine, others = lines(c * 64, 64), lines((1 - c) * 64, 64)
    strip = lines(c * 64 + x * 16, 16)

    def stage1(k):
        w, p0, p1, c0, c1 = batches[k]
        n = p1 - p0
        a = T[p0:p1].reshape(n * ROWS, FEAT)
        v = jnp.dot(a, W[w, :, c0:c1], preferred_element_type=f32)
        PP[w, p0:p1, :, c0:c1] = v.reshape(n, ROWS, c1 - c0)
        S1[w, p0:p1, :, c0:c1] = PP[w, p0:p1, others, c0:c1].astype(bf16)
        at = (w, pl.ds(p0, n), slice(None), pl.ds(c0, c1 - c0))
        in1[k] = net.put(S1.at[at], R1.at[at], core_peer)

    def stage2(k):
        w, p0, p1, c0, c1 = batches[k]
        at = (w, pl.ds(p0, p1 - p0), slice(None), pl.ds(c0, c1 - c0))
        net.got(in1[k], R1.at[at])
        PP[w, p0:p1, mine, c0:c1] += R1[w, p0:p1, :, c0:c1].astype(f32)
        for o in (1, 2, 3):
            rows = lines(c * 64 + x_to(o) * 16, 16)
            S2[o - 1, w, p0:p1, :, c0:c1] = PP[w, p0:p1, rows, c0:c1].astype(bf16)
            in2[k, o] = net.put(
                S2.at[(o - 1, *at)], R2.at[(o - 1, *at)], x_peer(o)
            )

    def stage3(k):
        w, p0, p1, c0, c1 = batches[k]
        at = (w, pl.ds(p0, p1 - p0), slice(None), pl.ds(c0, c1 - c0))
        v = PP[w, p0:p1, strip, c0:c1]
        for o in (1, 2, 3):
            net.got(in2[k, o], R2.at[(o - 1, *at)])
            v += R2[o - 1, w, p0:p1, :, c0:c1].astype(f32)
        S3[w, p0:p1, :, c0:c1] = v.astype(bf16)
        in3[k] = net.put(S3.at[at], R3.at[at], grp_peer)

    def stage4(k):
        w, p0, p1, c0, c1 = batches[k]
        at = (w, pl.ds(p0, p1 - p0), slice(None), pl.ds(c0, c1 - c0))
        net.got(in3[k], R3.at[at])
        v = S3[w, p0:p1, :, c0:c1].astype(f32) + R3[w, p0:p1, :, c0:c1].astype(f32)
        N[w, p0:p1, strip, c0:c1] = (v * G[w, 0:1, c0:c1]).astype(bf16)
        v = v * v
        fold = sum(v[:, :, i : i + 128] for i in range(0, c1 - c0, 128))
        for p in range(p0, p1):
            SA[at_z(DISTANCE[p])] += fold[p - p0]
        piece = N.at[w, pl.ds(p0, p1 - p0), strip, pl.ds(c0, c1 - c0)]
        for o in (1, 2, 3):
            inx[k, o] = net.put(piece, piece, x_peer(o))

    there, there_others = lines(ROWS + c * 64, 64), lines(ROWS + (1 - c) * 64, 64)

    def spread(*keys):
        for k in keys:
            w, p0, p1, c0, c1 = batches[k]
            blocks, cols = pl.ds(p0, p1 - p0), pl.ds(c0, c1 - c0)
            for o in (1, 2, 3):
                rows = lines(c * 64 + x_to(-o) * 16, 16)
                net.got(inx[k, o], N.at[w, blocks, rows, cols])
            piece = N.at[w, blocks, mine, cols]
            inc[k] = net.put(piece, piece, core_peer)

    def have_near():
        for k, handle in inc.items():
            w, p0, p1, c0, c1 = batches[k]
            net.got(handle, N.at[w, pl.ds(p0, p1 - p0), others, pl.ds(c0, c1 - c0)])

    def to_far(*keys):
        for k in keys:
            w, p0, p1, c0, c1 = batches[k]
            blocks, cols = pl.ds(p0, p1 - p0), pl.ds(c0, c1 - c0)
            iny[k] = net.put(
                N.at[w, blocks, mine, cols], N.at[1 - w, blocks, there, cols], y_other
            )

    def pass_far(*keys):
        for k in keys:
            w, p0, p1, c0, c1 = batches[k]
            piece = N.at[1 - w, pl.ds(p0, p1 - p0), there, pl.ds(c0, c1 - c0)]
            net.got(iny[k], piece)
            inf[k] = net.put(piece, piece, core_peer)

    def have_far():
        for k, handle in inf.items():
            w, p0, p1, c0, c1 = batches[k]
            blocks, cols = pl.ds(p0, p1 - p0), pl.ds(c0, c1 - c0)
            net.got(handle, N.at[1 - w, blocks, there_others, cols])

    wh_in = []

    def head_piece(i):
        rows = lines((1 - yl) * SHIFT + PIECES[i], PIECES[i + 1] - PIECES[i])
        to = WH.at[1, pl.ds(PIECES[i], PIECES[i + 1] - PIECES[i])]
        wh_in.append(net.put(w_head.at[rows], to, y_peer))

    ring_step(1, 0)
    merge_piece(3)
    ring_step(1, 1)
    merge_piece(4)
    keep_local[0].wait()
    keep_local[1].wait()
    stage1("a")
    stage2("a")
    ring_step(2, 0)
    merge_piece(5)
    stage3("a")
    ring_step(2, 1)
    merge_piece(6)
    stage1("b")
    ring_step(3, 0)
    merge_piece(7)
    stage2("b")
    net.got(gain_in, G.at[1])
    for i in range(4):
        got_merge(i)
    stage1("c")
    ring_step(3, 1)
    stage1("d")
    stage1("f")
    got_merge(4)
    got_merge(5)
    stage1("g")
    stage2("c")
    stage3("b")
    stage4("a")
    for k in ("d", "f", "g"):
        stage2(k)
    ring_step(4, 0)
    ring_step(4, 1)
    stage1("e")
    stage1("h")
    stage3("c")
    got_merge(6)
    got_merge(7)
    stage1("i")
    head_piece(0)
    stage2("e")
    stage2("h")
    for k in ("d", "f", "g"):
        stage3(k)
    stage2("i")
    stage4("b")
    spread("a")
    stage4("c")
    stage3("e")
    stage3("h")
    for k in ("d", "f", "g"):
        stage4(k)
    stage3("i")
    head_piece(1)
    stage4("e")
    stage4("h")
    spread("b")
    spread("c")
    to_far("ab", "c")
    spread("d", "f", "g")
    to_far("d", "f", "g")
    stage4("i")
    head_piece(2)
    head_piece(3)

    by_row = SA[...].reshape(ROWS, 128).T
    SQ[z] = jnp.broadcast_to(jnp.sum(by_row, axis=0, keepdims=True), (8, ROWS))
    square_in = {(way, 1): net.put(SQ.at[z], SQ.at[z], ring[way]) for way in (0, 1)}
    spread("e", "h", "i")
    to_far("e", "h", "i")
    half_labels = LA.at[pl.ds(yl * Z, Z)]
    y_labels = net.put(half_labels, half_labels, y_peer)
    keep_local[2].wait()
    have_near()

    def piece_of(v, far):
        rows = pl.ds(SPLIT[v], SPLIT[v + 1] - SPLIT[v])
        return rows, pl.ds(ROWS * far, ROWS)

    def logits_part(p, v, far, out):
        rows, lanes = piece_of(v, far)
        total = None
        for w in (0, 1):
            part = lax.dot_general(
                WH[w, rows, :],
                N[w, p, lanes, :],
                (((1,), (1,)), ((), ())),
                preferred_element_type=f32,
            )
            total = part if total is None else total + part
        out[rows, lanes] = total

    logit_in = {}

    def logits_step(*parts):
        for way, (s, v, far) in enumerate(parts):
            logits_part(POS[s if way == 0 else -s], v, far, PB.at[way])
        for way, (s, v, far) in enumerate(parts):
            at = piece_of(v, far)
            total = PB[(way, *at)]
            if (way, s + 1, v, far) in logit_in:
                net.got(logit_in[way, s + 1, v, far], ER.at[(way, s, *at)])
                total += ER[(way, s, *at)].astype(f32)
            ES[(way, s - 1, *at)] = total.astype(bf16)
            logit_in[way, s, v, far] = net.put(
                ES.at[(way, s - 1, *at)], ER.at[(way, s - 1, *at)], ring[way]
            )

    def got_head(i):
        net.got(wh_in[i], WH.at[1, pl.ds(PIECES[i], PIECES[i + 1] - PIECES[i])])

    got_head(0)
    got_head(1)
    def squares_step(s):
        for way in (0, 1):
            small_step(SQ, 0, square_in, way, s)

    logits_step((4, 0, 0), (3, 0, 0))
    logits_step((3, 0, 0), (2, 0, 0))
    squares_step(1)
    pass_far("ab", "c")
    got_head(2)
    got_head(3)
    logits_step((3, 1, 0), (4, 1, 0))
    pass_far("d")
    logits_step((2, 0, 0), (1, 0, 0))
    squares_step(2)
    pass_far("f", "g")
    logits_step((2, 1, 0), (3, 1, 0))
    pass_far("e", "h", "i")
    have_far()
    logits_step((4, 0, 1), (4, 1, 1))
    squares_step(3)
    logits_step((1, 0, 0), (2, 1, 0))
    logits_step((1, 1, 0), (3, 0, 1))
    squares_step(4)

    total = SQ[0]
    for i in range(1, Z):
        total += SQ[i]
    r = lax.rsqrt(total[0:1] / D + 1e-05)
    CB[...] = jnp.broadcast_to(r, (ROWS, ROWS)).T.reshape(8, 16, ROWS)
    for p in range(8):
        RC[0, p, strip, :] = CB[at_z(DISTANCE[p])]
    rx_in = [
        net.put(RC.at[0, :, strip], RC.at[0, :, strip], x_peer(o)) for o in (1, 2, 3)
    ]
    logits_step((3, 1, 1), (1, 1, 0))
    logits_step((3, 0, 1), (3, 1, 1))
    for o in (1, 2, 3):
        net.got(rx_in[o - 1], RC.at[0, :, lines(c * 64 + x_to(-o) * 16, 16)])
    rc_in = net.put(RC.at[0, :, mine], RC.at[0, :, mine], core_peer)
    ry_in = net.put(RC.at[0, :, mine], RC.at[1, :, mine], y_other)
    logits_step((2, 1, 1), (2, 0, 1))
    logits_step((2, 0, 1), (2, 1, 1))
    net.got(ry_in, RC.at[1, :, mine])
    rf_in = net.put(RC.at[1, :, mine], RC.at[1, :, mine], core_peer)
    logits_step((1, 1, 1), (1, 0, 1))
    logits_step((1, 0, 1), (1, 1, 1))
    net.got(rc_in, RC.at[0, :, others])
    net.got(rf_in, RC.at[1, :, others])

    side = lax.rem(g + yl, 2)
    away = lax.rem(t - z + Z, Z)
    far = lax.div(away, 5)
    p = (1 - far) * (2 * away - 1) + far * (16 - 2 * away) + lax.div(Z - away, Z)
    rows = lines(side * ROWS, ROWS)
    normed_out[...] = (N[0, p, rows, :].astype(f32) * RC[side, p][:, 0:1]).astype(bf16)

    net.got(y_labels, LA.at[pl.ds((1 - yl) * Z, Z)])
    domain = lax.broadcasted_iota(jnp.int32, (8, ROWS), 0)
    counts = jnp.zeros((8, ROWS), f32)
    for i in range(16):
        counts += jnp.where((LA[i] == domain) & (i < d), 1.0, 0.0)
    onehot = jnp.where(labels[...] == domain, 1.0, 0.0)
    earlier = jnp.where(
        lax.broadcasted_iota(jnp.int32, (ROWS, ROWS), 0)
        < lax.broadcasted_iota(jnp.int32, (ROWS, ROWS), 1),
        1.0,
        0.0,
    )
    before = jnp.dot(
        onehot.astype(bf16), earlier.astype(bf16), preferred_element_type=f32
    ) + jnp.sum(counts, axis=1, keepdims=True)
    rank = jnp.sum(onehot * before, axis=0, keepdims=True)
    allowed = jnp.zeros((1, ROWS), jnp.int32)
    for e in range(8):
        allowed = jnp.where(labels[...] == e, quotas[e], allowed)

    for v in (0, 1):
        for far in (0, 1):
            logits_part(0, v, far, PB.at[0])
    net.got(token_in, TK.at[1])
    scale = [RC[far, 0].T[0:1] for far in (0, 1)]
    first = (g * 8 + t) * VOC + yl * SHIFT
    def sums_of(v, far):
        for way in (0, 1):
            net.got(logit_in[way, 1, v, far], ER.at[(way, 0, *piece_of(v, far))])
        lanes = pl.ds(ROWS * far, ROWS)
        valid = yl * (2 * MINE - VOC)

        def summed(k, sums):
            start = SPLIT[v] + k * 48
            rows = pl.ds(pl.multiple_of(start, 16), 48)
            u = PB[0, rows, lanes] + ER[0, 0, rows, lanes].astype(f32)
            u = (u + ER[1, 0, rows, lanes].astype(f32)) * scale[far]
            row = start + lax.broadcasted_iota(jnp.int32, (48, ROWS), 0)
            counted = row >= valid
            hit = jnp.where(counted & (row + first == TK[far, 0:1]), u, 0.0)
            e = jnp.where(counted, jnp.exp(u), 0.0)
            return (
                sums[0] + jnp.sum(e.reshape(6, 8, ROWS), axis=0),
                sums[1] + jnp.sum(hit.reshape(6, 8, ROWS), axis=0),
            )

        zero = jnp.zeros((8, ROWS), f32)
        return lax.fori_loop(0, (SPLIT[v + 1] - SPLIT[v]) // 48, summed, (zero, zero))

    parts = {at: sums_of(*at) for at in ((1, 0), (0, 0), (0, 1), (1, 1))}
    pairs = []
    for far in (0, 1):
        sumexp, target = (
            jnp.sum(parts[0, far][i] + parts[1, far][i], axis=0, keepdims=True)
            for i in (0, 1)
        )
        pairs.append(jnp.where(domain < 4, sumexp, target))

    FR[c] = pairs[0]
    FB[0] = pairs[0]
    FB[1] = pairs[1]
    near = [
        net.put(FB.at[0], FR.at[c], core_peer),
        net.put(FB.at[1], FR.at[2 + c], y_peer),
        net.put(FB.at[1], FR.at[2 + c], y_core),
    ]
    net.got(near[0], FR.at[1 - c])
    net.got(near[1], FR.at[2 + c])
    net.got(near[2], FR.at[3 - c])
    pair = (FR[0] + FR[1]) + (FR[2] + FR[3])
    at = 4 + 4 * g
    FB[2] = pair
    FR[at + x] = pair
    across = [
        (net.put(FB.at[2], FR.at[at + x], {"grp": g if same else 1 - g, **x_peer(o)}), same, o)
        for same in (True, False)
        for o in range(4)
        if o or not same
    ]
    for handle, same, o in across:
        net.got(handle, FR.at[(at if same else 8 - 4 * g) + x_to(-o)])
    pair = (FR[4] + FR[5]) + (FR[6] + FR[7])
    pair += (FR[8] + FR[9]) + (FR[10] + FR[11])
    loss = jnp.log(pair[0:1]) - pair[4:5]
    loss_out[...] = jnp.where(rank < allowed.astype(f32), loss, 0.0)
    net.drain()


def on_device(tiers, w_merge, norm_gain, w_head, token_ids, labels, quotas):
    f32, bf16, i32 = jnp.float32, jnp.bfloat16, jnp.int32
    vmem = pl.BlockSpec(memory_space=pltpu.VMEM)
    hbm = pl.BlockSpec(memory_space=pl.ANY)
    normed, loss = pl.pallas_call(
        kernel,
        out_shape=(
            jax.ShapeDtypeStruct((ROWS, COLS), bf16),
            jax.ShapeDtypeStruct((1, ROWS), f32),
        ),
        in_specs=[
            hbm, hbm, vmem, hbm, vmem, vmem, pl.BlockSpec(memory_space=pltpu.SMEM),
        ],
        out_specs=(vmem, vmem),
        scratch_shapes=[
            pltpu.VMEM((8, ROWS, FEAT), bf16),
            pltpu.VMEM((2, FEAT, COLS), bf16),
            pltpu.VMEM((2, 8, COLS), f32),
            pltpu.VMEM((2, 8, ROWS), i32),
            pltpu.VMEM((2, MINE, COLS), bf16),
            pltpu.VMEM((16, 8, ROWS), i32),
            pltpu.VMEM((2, 8, 64, COLS), bf16),
            pltpu.VMEM((2, 8, 64, COLS), bf16),
            pltpu.VMEM((2, 8, ROWS, COLS), f32),
            pltpu.VMEM((3, 2, 8, 16, COLS), bf16),
            pltpu.VMEM((3, 2, 8, 16, COLS), bf16),
            pltpu.VMEM((2, 8, 16, COLS), bf16),
            pltpu.VMEM((2, 8, 16, COLS), bf16),
            pltpu.VMEM((8, 16, 128), f32),
            pltpu.VMEM((Z, 8, ROWS), f32),
            pltpu.VMEM((8, 16, ROWS), f32),
            pltpu.VMEM((2, 8, ROWS, 128), f32),
            pltpu.VMEM((2, 8, 2 * ROWS, COLS), bf16),
            pltpu.VMEM((2, 4, MINE, 2 * ROWS), bf16),
            pltpu.VMEM((2, 4, MINE, 2 * ROWS), bf16),
            pltpu.VMEM((2, MINE, 2 * ROWS), f32),
            pltpu.VMEM((3, 8, ROWS), f32),
            pltpu.VMEM((12, 8, ROWS), f32),
            pltpu.SemaphoreType.DMA((N_SEMS,)),
            pltpu.SemaphoreType.DMA((N_SEMS,)),
            pltpu.SemaphoreType.DMA((3,)),
        ],
        compiler_params=pltpu.CompilerParams(
            collective_id=0, has_side_effects=True, vmem_limit_bytes=56 * 2**20
        ),
    )(
        tiers,
        w_merge,
        norm_gain.reshape(1, COLS),
        w_head.T,
        token_ids.reshape(1, ROWS),
        labels.reshape(1, ROWS),
        quotas,
    )
    return normed, loss.reshape(ROWS)


def solution(mesh):
    both = ("grp", "tp")
    in_specs = (
        P("dp", both),
        P(both, "dp"),
        P("dp"),
        P("dp", both),
        P("dp"),
        P("dp"),
        P(),
    )
    out_specs = (P(both, "dp"), P("dp"))
    return jax.shard_map(
        on_device, mesh=mesh, in_specs=in_specs, out_specs=out_specs, check_vma=False
    )
```

```python
import jax
import jax.numpy as jnp
from jax import lax
from jax.experimental import pallas as pl
from jax.experimental.pallas import tpu as pltpu
from jax.sharding import PartitionSpec as P

D = 8192
Z = 8
ROWS = 128
FEAT = 1536
COLS = 512
VOC = 2000
MINE = 1008
SHIFT = VOC - MINE
SPLIT = (0, 528, MINE)
PIECES = (0, 144, 528, 768, MINE)
N_SEMS = 200
DISTANCE = (0, 1, -1, 2, -2, 3, -3, 4)
POS = {s: i for i, s in enumerate(DISTANCE)} | {-4: 7}


class Net:
    def __init__(self, send, recv):
        self.send, self.recv, self.n, self.started = send, recv, 0, {}

    def make(self, src, dst, device, i):
        return pltpu.make_async_remote_copy(
            src_ref=src,
            dst_ref=dst,
            send_sem=self.send.at[i],
            recv_sem=self.recv.at[i],
            device_id=device,
            device_id_type=pl.DeviceIdType.MESH,
        )

    def put(self, src, dst, device):
        i = self.n
        self.n += 1
        assert i < N_SEMS
        copy = self.make(src, dst, device, i)
        copy.start()
        self.started[i] = copy
        return i, device

    def got(self, handle, dst):
        i, device = handle
        self.make(dst, dst, device, i).wait_recv()

    def sent(self, handles):
        for i, _ in handles:
            self.started.pop(i).wait_send()

    def drain(self):
        for copy in self.started.values():
            copy.wait_send()


def kernel(
    tiers, w_merge, gain, w_head, token_ids, labels, quotas,
    normed_out, loss_out,
    T, W, G, TK, WH, LA, S1, R1, PP, S2, R2, S3, R3, SA, SQ, CB, RC, N, ES, ER, PB, FB, FR,
    send, recv, local,
):
    f32, bf16 = jnp.float32, jnp.bfloat16
    g, d, t = (lax.axis_index(a) for a in ("grp", "dp", "tp"))
    yl, z = lax.div(d, Z), lax.rem(d, Z)
    x, c = lax.div(t, 2), lax.rem(t, 2)
    net = Net(send, recv)

    def at_z(step):
        return lax.rem(z + step + 2 * Z, Z)

    ring = [{"dp": yl * Z + at_z(1)}, {"dp": yl * Z + at_z(-1)}]
    y_peer = {"dp": (1 - yl) * Z + z}
    y_other = {"grp": 1 - g, "dp": (1 - yl) * Z + z}
    core_peer = {"tp": 2 * x + 1 - c}
    grp_peer = {"grp": 1 - g}

    def x_to(o):
        return lax.rem(x + o + 4, 4)

    def x_peer(o):
        return {"tp": 2 * x_to(o) + c}

    def lines(start, size):
        return pl.ds(pl.multiple_of(start, 16), size)

    barrier = pltpu.get_barrier_semaphore()
    y_core = {"dp": (1 - yl) * Z + z, "tp": 2 * x + 1 - c}
    peers = [core_peer, grp_peer, y_other, y_core]
    peers += [{"grp": 1 - g, **x_peer(o)} for o in (1, 2, 3)]
    peers += [x_peer(o) for o in (1, 2, 3)] + [*ring, y_peer]
    for peer in peers:
        pl.semaphore_signal(
            barrier, inc=1, device_id=peer, device_id_type=pl.DeviceIdType.MESH
        )
    own_head = w_head.at[lines(yl * SHIFT, MINE)]
    keep_local = [
        pltpu.make_async_copy(tiers, T.at[0], local.at[0]),
        pltpu.make_async_copy(w_merge, W.at[0], local.at[1]),
        pltpu.make_async_copy(own_head, WH.at[0], local.at[2]),
    ]
    for copy in keep_local:
        copy.start()
    G[0] = jnp.broadcast_to(gain[...], (8, COLS))
    TK[0] = jnp.broadcast_to(token_ids[...], (8, ROWS))
    LA[d] = jnp.broadcast_to(labels[...], (8, ROWS))
    SA[...] = jnp.zeros_like(SA)
    pl.semaphore_wait(barrier, len(peers))

    def half(h):
        return pl.ds(64 * h, 64)

    def from_way(way, s):
        return POS[-s if way == 0 else s]

    tier_in = {}
    for h in (0, 1):
        for way in (0, 1):
            tier_in[way, 1, h] = net.put(
                tiers.at[half(h)], T.at[from_way(way, 1), half(h)], ring[way]
            )
    w_in = []

    def merge_part(i):
        return pl.ds(768 * (i % 2), 768), pl.ds(128 * (i // 2), 128)

    def merge_piece(i):
        rows, cols = merge_part(i)
        w_in.append(net.put(w_merge.at[rows, cols], W.at[1, rows, cols], y_peer))

    def got_merge(i):
        net.got(w_in[i], W.at[(1, *merge_part(i))])

    for i in range(3):
        merge_piece(i)
    gain_in = net.put(G.at[0], G.at[1], y_peer)
    token_in = net.put(TK.at[0], TK.at[1], y_peer)
    label_in = {(way, 1): net.put(LA.at[d], LA.at[d], ring[way]) for way in (0, 1)}

    def small_step(buf, first, handles, way, s):
        if (way, s) in handles:
            piece = buf.at[first + at_z(-s if way == 0 else s)]
            net.got(handles[way, s], piece)
            if s < 3 or (s == 3 and way == 0):
                handles[way, s + 1] = net.put(piece, piece, ring[way])

    def ring_step(s, h):
        for way in (0, 1):
            if (way, s, h) in tier_in:
                piece = T.at[from_way(way, s), half(h)]
                net.got(tier_in[way, s, h], piece)
                if s < 3 or (s == 3 and h == way):
                    to = T.at[from_way(way, s + 1), half(h)]
                    tier_in[way, s + 1, h] = net.put(piece, to, ring[way])
        small_step(LA, yl * Z, label_in, h, s)

    batches = {
        "a": (0, 0, 3, 0, COLS),
        "b": (0, 3, 5, 0, COLS),
        "c": (1, 0, 5, 0, 256),
        "d": (0, 5, 7, 0, COLS),
        "e": (0, 7, 8, 0, COLS),
        "f": (1, 5, 7, 0, 256),
        "g": (1, 0, 7, 256, 384),
        "h": (1, 7, 8, 0, 384),
        "i": (1, 0, 8, 384, COLS),
        "ab": (0, 0, 5, 0, COLS),
    }
    in1, in2, in3, inx, inc, iny, inf = {}, {}, {}, {}, {}, {}, {}
    mine, others = lines(c * 64, 64), lines((1 - c) * 64, 64)
    strip = lines(c * 64 + x * 16, 16)

    def stage1(k):
        w, p0, p1, c0, c1 = batches[k]
        n = p1 - p0
        a = T[p0:p1].reshape(n * ROWS, FEAT)
        v = jnp.dot(a, W[w, :, c0:c1], preferred_element_type=f32)
        PP[w, p0:p1, :, c0:c1] = v.reshape(n, ROWS, c1 - c0)
        S1[w, p0:p1, :, c0:c1] = PP[w, p0:p1, others, c0:c1].astype(bf16)
        at = (w, pl.ds(p0, n), slice(None), pl.ds(c0, c1 - c0))
        in1[k] = net.put(S1.at[at], R1.at[at], core_peer)

    def stage2(k):
        w, p0, p1, c0, c1 = batches[k]
        at = (w, pl.ds(p0, p1 - p0), slice(None), pl.ds(c0, c1 - c0))
        net.got(in1[k], R1.at[at])
        PP[w, p0:p1, mine, c0:c1] += R1[w, p0:p1, :, c0:c1].astype(f32)
        for o in (1, 2, 3):
            rows = lines(c * 64 + x_to(o) * 16, 16)
            S2[o - 1, w, p0:p1, :, c0:c1] = PP[w, p0:p1, rows, c0:c1].astype(bf16)
            in2[k, o] = net.put(
                S2.at[(o - 1, *at)], R2.at[(o - 1, *at)], x_peer(o)
            )

    def stage3(k):
        w, p0, p1, c0, c1 = batches[k]
        at = (w, pl.ds(p0, p1 - p0), slice(None), pl.ds(c0, c1 - c0))
        v = PP[w, p0:p1, strip, c0:c1]
        for o in (1, 2, 3):
            net.got(in2[k, o], R2.at[(o - 1, *at)])
            v += R2[o - 1, w, p0:p1, :, c0:c1].astype(f32)
        S3[w, p0:p1, :, c0:c1] = v.astype(bf16)
        in3[k] = net.put(S3.at[at], R3.at[at], grp_peer)

    def stage4(k):
        w, p0, p1, c0, c1 = batches[k]
        at = (w, pl.ds(p0, p1 - p0), slice(None), pl.ds(c0, c1 - c0))
        net.got(in3[k], R3.at[at])
        v = S3[w, p0:p1, :, c0:c1].astype(f32) + R3[w, p0:p1, :, c0:c1].astype(f32)
        N[w, p0:p1, strip, c0:c1] = (v * G[w, 0:1, c0:c1]).astype(bf16)
        v = v * v
        fold = sum(v[:, :, i : i + 128] for i in range(0, c1 - c0, 128))
        for p in range(p0, p1):
            SA[at_z(DISTANCE[p])] += fold[p - p0]
        piece = N.at[w, pl.ds(p0, p1 - p0), strip, pl.ds(c0, c1 - c0)]
        for o in (1, 2, 3):
            inx[k, o] = net.put(piece, piece, x_peer(o))

    there, there_others = lines(ROWS + c * 64, 64), lines(ROWS + (1 - c) * 64, 64)

    def spread(*keys):
        for k in keys:
            w, p0, p1, c0, c1 = batches[k]
            blocks, cols = pl.ds(p0, p1 - p0), pl.ds(c0, c1 - c0)
            for o in (1, 2, 3):
                rows = lines(c * 64 + x_to(-o) * 16, 16)
                net.got(inx[k, o], N.at[w, blocks, rows, cols])
            piece = N.at[w, blocks, mine, cols]
            inc[k] = net.put(piece, piece, core_peer)

    def have_near():
        for k, handle in inc.items():
            w, p0, p1, c0, c1 = batches[k]
            net.got(handle, N.at[w, pl.ds(p0, p1 - p0), others, pl.ds(c0, c1 - c0)])

    def to_far(*keys):
        for k in keys:
            w, p0, p1, c0, c1 = batches[k]
            blocks, cols = pl.ds(p0, p1 - p0), pl.ds(c0, c1 - c0)
            iny[k] = net.put(
                N.at[w, blocks, mine, cols], N.at[1 - w, blocks, there, cols], y_other
            )

    def pass_far(*keys):
        for k in keys:
            w, p0, p1, c0, c1 = batches[k]
            piece = N.at[1 - w, pl.ds(p0, p1 - p0), there, pl.ds(c0, c1 - c0)]
            net.got(iny[k], piece)
            inf[k] = net.put(piece, piece, core_peer)

    def have_far():
        for k, handle in inf.items():
            w, p0, p1, c0, c1 = batches[k]
            blocks, cols = pl.ds(p0, p1 - p0), pl.ds(c0, c1 - c0)
            net.got(handle, N.at[1 - w, blocks, there_others, cols])

    wh_in = []

    def head_piece(i):
        rows = lines((1 - yl) * SHIFT + PIECES[i], PIECES[i + 1] - PIECES[i])
        to = WH.at[1, pl.ds(PIECES[i], PIECES[i + 1] - PIECES[i])]
        wh_in.append(net.put(w_head.at[rows], to, y_peer))

    ring_step(1, 0)
    merge_piece(3)
    ring_step(1, 1)
    merge_piece(4)
    keep_local[0].wait()
    keep_local[1].wait()
    stage1("a")
    stage2("a")
    ring_step(2, 0)
    merge_piece(5)
    stage3("a")
    ring_step(2, 1)
    merge_piece(6)
    stage1("b")
    ring_step(3, 0)
    merge_piece(7)
    stage2("b")
    net.got(gain_in, G.at[1])
    for i in range(4):
        got_merge(i)
    stage1("c")
    ring_step(3, 1)
    stage1("d")
    stage1("f")
    got_merge(4)
    got_merge(5)
    stage1("g")
    stage2("c")
    stage3("b")
    stage4("a")
    for k in ("d", "f", "g"):
        stage2(k)
    ring_step(4, 0)
    ring_step(4, 1)
    stage1("e")
    stage1("h")
    stage3("c")
    got_merge(6)
    got_merge(7)
    stage1("i")
    head_piece(0)
    stage2("e")
    stage2("h")
    for k in ("d", "f", "g"):
        stage3(k)
    stage2("i")
    stage4("b")
    spread("a")
    stage4("c")
    stage3("e")
    stage3("h")
    for k in ("d", "f", "g"):
        stage4(k)
    stage3("i")
    head_piece(1)
    stage4("e")
    stage4("h")
    spread("b")
    spread("c")
    to_far("ab", "c")
    spread("d", "f", "g")
    to_far("d", "f", "g")
    stage4("i")
    head_piece(2)
    head_piece(3)

    spread("e", "h", "i")
    to_far("e", "h", "i")
    half_labels = LA.at[pl.ds(yl * Z, Z)]
    y_labels = net.put(half_labels, half_labels, y_peer)
    keep_local[2].wait()

    by_row = SA[...].reshape(ROWS, 128).T
    SQ[z] = jnp.broadcast_to(jnp.sum(by_row, axis=0, keepdims=True), (8, ROWS))
    square_in = {(way, 1): net.put(SQ.at[z], SQ.at[z], ring[way]) for way in (0, 1)}
    have_near()

    def piece_of(v, far):
        rows = pl.ds(SPLIT[v], SPLIT[v + 1] - SPLIT[v])
        return rows, pl.ds(ROWS * far, ROWS)

    def logits_part(p, v, far, out):
        rows, lanes = piece_of(v, far)
        total = None
        for w in (0, 1):
            part = lax.dot_general(
                WH[w, rows, :],
                N[w, p, lanes, :],
                (((1,), (1,)), ((), ())),
                preferred_element_type=f32,
            )
            total = part if total is None else total + part
        out[rows, lanes] = total

    logit_in = {}

    def logits_step(*parts):
        for way, (s, v, far) in enumerate(parts):
            logits_part(POS[s if way == 0 else -s], v, far, PB.at[way])
        for way, (s, v, far) in enumerate(parts):
            at = piece_of(v, far)
            total = PB[(way, *at)]
            if (way, s + 1, v, far) in logit_in:
                net.got(logit_in[way, s + 1, v, far], ER.at[(way, s, *at)])
                total += ER[(way, s, *at)].astype(f32)
            ES[(way, s - 1, *at)] = total.astype(bf16)
            logit_in[way, s, v, far] = net.put(
                ES.at[(way, s - 1, *at)], ER.at[(way, s - 1, *at)], ring[way]
            )

    def got_head(i):
        net.got(wh_in[i], WH.at[1, pl.ds(PIECES[i], PIECES[i + 1] - PIECES[i])])

    got_head(0)
    got_head(1)
    def squares_step(s):
        for way in (0, 1):
            small_step(SQ, 0, square_in, way, s)

    logits_step((4, 0, 0), (3, 0, 0))
    logits_step((3, 0, 0), (2, 0, 0))
    squares_step(1)
    pass_far("ab", "c")
    got_head(2)
    got_head(3)
    logits_step((3, 1, 0), (4, 1, 0))
    pass_far("d")
    logits_step((2, 0, 0), (1, 0, 0))
    squares_step(2)
    pass_far("f", "g")
    logits_step((2, 1, 0), (3, 1, 0))
    pass_far("e", "h", "i")
    have_far()
    logits_step((4, 0, 1), (4, 1, 1))
    squares_step(3)
    logits_step((1, 0, 0), (2, 1, 0))
    logits_step((1, 1, 0), (3, 0, 1))
    squares_step(4)

    total = SQ[0]
    for i in range(1, Z):
        total += SQ[i]
    r = lax.rsqrt(total[0:1] / D + 1e-05)
    CB[...] = jnp.broadcast_to(r, (ROWS, ROWS)).T.reshape(8, 16, ROWS)
    for p in range(8):
        RC[0, p, strip, :] = CB[at_z(DISTANCE[p])]
    rx_in = [
        net.put(RC.at[0, :, strip], RC.at[0, :, strip], x_peer(o)) for o in (1, 2, 3)
    ]
    logits_step((3, 1, 1), (1, 1, 0))
    logits_step((3, 0, 1), (3, 1, 1))
    for o in (1, 2, 3):
        net.got(rx_in[o - 1], RC.at[0, :, lines(c * 64 + x_to(-o) * 16, 16)])
    rc_in = net.put(RC.at[0, :, mine], RC.at[0, :, mine], core_peer)
    ry_in = net.put(RC.at[0, :, mine], RC.at[1, :, mine], y_other)
    logits_step((2, 1, 1), (2, 0, 1))
    logits_step((2, 0, 1), (2, 1, 1))
    net.got(ry_in, RC.at[1, :, mine])
    rf_in = net.put(RC.at[1, :, mine], RC.at[1, :, mine], core_peer)
    logits_step((1, 1, 1), (1, 0, 1))
    logits_step((1, 0, 1), (1, 1, 1))
    net.got(rc_in, RC.at[0, :, others])
    net.got(rf_in, RC.at[1, :, others])

    side = lax.rem(g + yl, 2)
    away = lax.rem(t - z + Z, Z)
    far = lax.div(away, 5)
    p = (1 - far) * (2 * away - 1) + far * (16 - 2 * away) + lax.div(Z - away, Z)
    rows = lines(side * ROWS, ROWS)
    normed_out[...] = (N[0, p, rows, :].astype(f32) * RC[side, p][:, 0:1]).astype(bf16)

    net.got(y_labels, LA.at[pl.ds((1 - yl) * Z, Z)])
    domain = lax.broadcasted_iota(jnp.int32, (8, ROWS), 0)
    counts = jnp.zeros((8, ROWS), f32)
    for i in range(16):
        counts += jnp.where((LA[i] == domain) & (i < d), 1.0, 0.0)
    onehot = jnp.where(labels[...] == domain, 1.0, 0.0)
    earlier = jnp.where(
        lax.broadcasted_iota(jnp.int32, (ROWS, ROWS), 0)
        < lax.broadcasted_iota(jnp.int32, (ROWS, ROWS), 1),
        1.0,
        0.0,
    )
    before = jnp.dot(
        onehot.astype(bf16), earlier.astype(bf16), preferred_element_type=f32
    ) + jnp.sum(counts, axis=1, keepdims=True)
    rank = jnp.sum(onehot * before, axis=0, keepdims=True)
    allowed = jnp.zeros((1, ROWS), jnp.int32)
    for e in range(8):
        allowed = jnp.where(labels[...] == e, quotas[e], allowed)

    for v in (0, 1):
        for far in (0, 1):
            logits_part(0, v, far, PB.at[0])
    net.got(token_in, TK.at[1])
    scale = [RC[far, 0].T[0:1] for far in (0, 1)]
    first = (g * 8 + t) * VOC + yl * SHIFT
    def sums_of(v, far):
        for way in (0, 1):
            net.got(logit_in[way, 1, v, far], ER.at[(way, 0, *piece_of(v, far))])
        lanes = pl.ds(ROWS * far, ROWS)
        valid = yl * (2 * MINE - VOC)

        def summed(k, sums):
            start = SPLIT[v] + k * 48
            rows = pl.ds(pl.multiple_of(start, 16), 48)
            u = PB[0, rows, lanes] + ER[0, 0, rows, lanes].astype(f32)
            u = (u + ER[1, 0, rows, lanes].astype(f32)) * scale[far]
            row = start + lax.broadcasted_iota(jnp.int32, (48, ROWS), 0)
            counted = row >= valid
            hit = jnp.where(counted & (row + first == TK[far, 0:1]), u, 0.0)
            e = jnp.where(counted, jnp.exp(u), 0.0)
            return (
                sums[0] + jnp.sum(e.reshape(6, 8, ROWS), axis=0),
                sums[1] + jnp.sum(hit.reshape(6, 8, ROWS), axis=0),
            )

        zero = jnp.zeros((8, ROWS), f32)
        return lax.fori_loop(0, (SPLIT[v + 1] - SPLIT[v]) // 48, summed, (zero, zero))

    parts = {at: sums_of(*at) for at in ((1, 0), (0, 0), (0, 1), (1, 1))}
    pairs = []
    for far in (0, 1):
        sumexp, target = (
            jnp.sum(parts[0, far][i] + parts[1, far][i], axis=0, keepdims=True)
            for i in (0, 1)
        )
        pairs.append(jnp.where(domain < 4, sumexp, target))

    FR[c] = pairs[0]
    FB[0] = pairs[0]
    FB[1] = pairs[1]
    near = [
        net.put(FB.at[0], FR.at[c], core_peer),
        net.put(FB.at[1], FR.at[2 + c], y_peer),
        net.put(FB.at[1], FR.at[2 + c], y_core),
    ]
    net.got(near[0], FR.at[1 - c])
    net.got(near[1], FR.at[2 + c])
    net.got(near[2], FR.at[3 - c])
    pair = (FR[0] + FR[1]) + (FR[2] + FR[3])
    at = 4 + 4 * g
    FB[2] = pair
    FR[at + x] = pair
    across = [
        (net.put(FB.at[2], FR.at[at + x], {"grp": g if same else 1 - g, **x_peer(o)}), same, o)
        for same in (True, False)
        for o in range(4)
        if o or not same
    ]
    for handle, same, o in across:
        net.got(handle, FR.at[(at if same else 8 - 4 * g) + x_to(-o)])
    pair = (FR[4] + FR[5]) + (FR[6] + FR[7])
    pair += (FR[8] + FR[9]) + (FR[10] + FR[11])
    loss = jnp.log(pair[0:1]) - pair[4:5]
    loss_out[...] = jnp.where(rank < allowed.astype(f32), loss, 0.0)
    net.drain()


def on_device(tiers, w_merge, norm_gain, w_head, token_ids, labels, quotas):
    f32, bf16, i32 = jnp.float32, jnp.bfloat16, jnp.int32
    vmem = pl.BlockSpec(memory_space=pltpu.VMEM)
    hbm = pl.BlockSpec(memory_space=pl.ANY)
    normed, loss = pl.pallas_call(
        kernel,
        out_shape=(
            jax.ShapeDtypeStruct((ROWS, COLS), bf16),
            jax.ShapeDtypeStruct((1, ROWS), f32),
        ),
        in_specs=[
            hbm, hbm, vmem, hbm, vmem, vmem, pl.BlockSpec(memory_space=pltpu.SMEM),
        ],
        out_specs=(vmem, vmem),
        scratch_shapes=[
            pltpu.VMEM((8, ROWS, FEAT), bf16),
            pltpu.VMEM((2, FEAT, COLS), bf16),
            pltpu.VMEM((2, 8, COLS), f32),
            pltpu.VMEM((2, 8, ROWS), i32),
            pltpu.VMEM((2, MINE, COLS), bf16),
            pltpu.VMEM((16, 8, ROWS), i32),
            pltpu.VMEM((2, 8, 64, COLS), bf16),
            pltpu.VMEM((2, 8, 64, COLS), bf16),
            pltpu.VMEM((2, 8, ROWS, COLS), f32),
            pltpu.VMEM((3, 2, 8, 16, COLS), bf16),
            pltpu.VMEM((3, 2, 8, 16, COLS), bf16),
            pltpu.VMEM((2, 8, 16, COLS), bf16),
            pltpu.VMEM((2, 8, 16, COLS), bf16),
            pltpu.VMEM((8, 16, 128), f32),
            pltpu.VMEM((Z, 8, ROWS), f32),
            pltpu.VMEM((8, 16, ROWS), f32),
            pltpu.VMEM((2, 8, ROWS, 128), f32),
            pltpu.VMEM((2, 8, 2 * ROWS, COLS), bf16),
            pltpu.VMEM((2, 4, MINE, 2 * ROWS), bf16),
            pltpu.VMEM((2, 4, MINE, 2 * ROWS), bf16),
            pltpu.VMEM((2, MINE, 2 * ROWS), f32),
            pltpu.VMEM((3, 8, ROWS), f32),
            pltpu.VMEM((12, 8, ROWS), f32),
            pltpu.SemaphoreType.DMA((N_SEMS,)),
            pltpu.SemaphoreType.DMA((N_SEMS,)),
            pltpu.SemaphoreType.DMA((3,)),
        ],
        compiler_params=pltpu.CompilerParams(
            collective_id=0, has_side_effects=True, vmem_limit_bytes=56 * 2**20
        ),
    )(
        tiers,
        w_merge,
        norm_gain.reshape(1, COLS),
        w_head.T,
        token_ids.reshape(1, ROWS),
        labels.reshape(1, ROWS),
        quotas,
    )
    return normed, loss.reshape(ROWS)


def solution(mesh):
    both = ("grp", "tp")
    in_specs = (
        P("dp", both),
        P(both, "dp"),
        P("dp"),
        P("dp", both),
        P("dp"),
        P("dp"),
        P(),
    )
    out_specs = (P(both, "dp"), P("dp"))
    return jax.shard_map(
        on_device, mesh=mesh, in_specs=in_specs, out_specs=out_specs, check_vma=False
    )
```
